128 devices in a mesh: tm: 2 (over core), space: 64 (over x, y, z).
Axes of the slice: x: 4, y: 4, z: 4, core: 2. Of those that a mesh axis runs over, the one named last changes fastest.
Arguments:
- winds: bfloat16 [4, 64, 2, 3, 384, 128], P('tm', 'space'), may hold values from -0.44921875 to 0.44921875
- mixing: float32 [128, 128], replicated, may hold values from -0.5 to 0.5
- innovations: float32 [2, 64, 64, 8, 384], P('tm', 'space'), may hold values from -6 to 6
- obs_weight: float32 [2, 64, 64, 8, 384], P('tm', 'space'), may hold values from 0.3 to 3
- obs_sub: int32 [2, 64, 64, 8], P('tm', 'space'), may hold values from 0 to 1
- obs_col: int32 [2, 64, 64, 8], P('tm', 'space'), may hold values from 0 to 1151
- obs_count: int32 [2, 64, 64], P('tm', 'space'), may hold values from 1 to 8, as said below
Outputs:
- increment: float32 [4, 64, 3, 3, 384, 128], P('tm', 'space')
- residual: float32 [4, 64, 3, 3, 384, 128], P('tm', 'space')
The draws below stay inside these ranges and needn't reach their ends.
Inputs may be any that keep to these rules, and one draw needn't show every extreme that they name: `obs_count`: slots at or above the count are empty; in every draw some owner of each group receives 8 live slots from every observer.
All inputs are finite; a program needn't handle non-finite values.
Results may differ from the reference program's by a relative error of at most 0.022.
Values sent between devices are 32-bit elements; how exact they have to be, the bound alone decides.
No kernel may reach another device: no remote copies, remote signals or barrier semaphores. Data moves between devices by JAX's collectives and lax.ppermute only.
A program may use at most 128 MiB of HBM per device.

```python
import math
import jax
import jax.numpy as jnp
from jax import lax

FIELDS = 3
LEV = 128
NLON = 384
TLAT = 3
SUB_DEV = 2
PER = 8
ITERS = 2
TLON = 384
PXT = 1
NLAT = 192
SUBW = 4
PROF = 384
CELLS = 1152
N_TM = 2
N_SPACE = 64


def draw_obs_count(key, part):
    first_key = jax.random.fold_in(key, 11)
    second_key = jax.random.fold_in(key, 23)
    base_counts = jax.random.randint(first_key, (N_TM, N_SPACE, N_SPACE), 1, PER + 1)
    full_owner = jax.random.randint(second_key, (N_TM,), 0, N_SPACE)
    owner_ids = jnp.arange(N_SPACE, dtype=jnp.int32)
    filled = owner_ids[None, None, :] == full_owner[:, None, None]
    return jnp.where(filled, PER, base_counts).astype(jnp.int32)


def touch_ends(values, stream_key, smallest, high):
    longest = values.shape.index(max(values.shape))
    spots = []
    for shift in (0, 1):
        where = [jax.random.randint(jax.random.fold_in(stream_key, axis), (), 0, length) for axis, length in enumerate(values.shape)]
        where[longest] = (where[longest] + shift) % values.shape[longest]
        spots.append(tuple(where))
    return values.at[spots[0]].set(smallest).at[spots[1]].set(high)


def block_scale(rng, extent, split, low, top_value):
    def one(position, parts):
        heights = jax.random.uniform(jax.random.fold_in(jax.random.fold_in(rng, 6), position), (parts,), jnp.float32, low / len(split), top_value / len(split))
        return jnp.repeat(jnp.exp(heights), extent[position] // parts).reshape((-1,) + (1,) * (len(extent) - position - 1))

    factor_of = one(*split[0])
    for cut in split[1:]:
        factor_of = factor_of * one(*cut)
    return factor_of


def noise(stream_key, extent, width, bound, split=(), kind=jnp.bfloat16):
    array = jax.random.normal(stream_key, extent, jnp.float32) * width
    if len(split) > 0:
        array = block_scale(stream_key, extent, split, -0.22, 0.18) * array
    return jnp.clip(array, min=-bound, max=bound).astype(kind)


def setup_inputs(seed: int = 0) -> dict:
    arg_keys = jax.random.split(jax.random.key(seed), 8)
    return {
        "winds": jnp.clip(jax.random.uniform(arg_keys[0], (SUBW, N_SPACE, 2, TLAT, TLON, LEV), jnp.float32, -0.44921875, 0.44921875) * block_scale(arg_keys[0], (SUBW, N_SPACE, 2, TLAT, TLON, LEV), ((0, 2), (1, 64)), -0.4, 0.0), -0.44921875, 0.44921875).astype(jnp.bfloat16),
        "mixing": noise(arg_keys[1], (LEV, LEV), LEV ** -0.5, 0.5, (), jnp.float32),
        "innovations": noise(arg_keys[2], (N_TM, N_SPACE, N_SPACE, PER, PROF), 1.0, 6.0, ((0, 2), (1, 64)), jnp.float32),
        "obs_weight": jnp.clip(jnp.exp(math.log(3.0) - 2.3025851 * jax.random.uniform(arg_keys[3], (N_TM, N_SPACE, N_SPACE, PER, PROF), jnp.float32) ** block_scale(arg_keys[3], (N_TM, N_SPACE, N_SPACE, PER, PROF), ((0, 2), (1, 64)), -0.2, 0.2)), 0.3, 3.0),
        "obs_sub": touch_ends(jax.random.randint(arg_keys[4], (N_TM, N_SPACE, N_SPACE, PER), 0, SUB_DEV), jax.random.fold_in(arg_keys[4], 1), 0, SUB_DEV - 1).astype(jnp.int32),
        "obs_col": touch_ends(jax.random.randint(arg_keys[5], (N_TM, N_SPACE, N_SPACE, PER), 0, CELLS), jax.random.fold_in(arg_keys[5], 1), 0, CELLS - 1).astype(jnp.int32),
        "obs_count": draw_obs_count(jax.random.fold_in(arg_keys[7], 71), 0),
    }


MIXC = 0.25
SCALE_B = 1.0
SCALE_Q = 0.5

def untile(tiled):
    lead = tiled.shape[0]
    comps = tiled.shape[2]
    rows_tiles = N_SPACE // PXT
    shaped = tiled.reshape(lead, rows_tiles, PXT, comps, TLAT, TLON, LEV)
    return shaped.transpose(0, 3, 1, 4, 2, 5, 6).reshape(lead, comps, NLAT, NLON, LEV)

def retile(full_grid):
    lead = full_grid.shape[0]
    comps = full_grid.shape[1]
    rows_tiles = N_SPACE // PXT
    shaped = full_grid.reshape(lead, comps, rows_tiles, TLAT, PXT, TLON, LEV)
    return shaped.transpose(0, 2, 4, 1, 3, 5, 6).reshape(lead, N_SPACE, comps, TLAT, TLON, LEV)

def moved(padded, wind_pair, mixing):
    values = padded[:, 1:-1]
    zonal_courant = wind_pair[0:1].astype(jnp.float32)
    merid_courant = wind_pair[1:2].astype(jnp.float32)
    westward = jnp.roll(values, 1, axis=2)
    eastward = jnp.roll(values, -1, axis=2)
    southern = padded[:, :-2]
    northern = padded[:, 2:]
    result = values - jnp.maximum(zonal_courant, 0.0) * (values - westward)
    result = result - jnp.maximum(-zonal_courant, 0.0) * (values - eastward)
    result = result - jnp.maximum(merid_courant, 0.0) * (values - southern)
    result = result - jnp.maximum(-merid_courant, 0.0) * (values - northern)
    return result + MIXC * jnp.einsum('aijl,kl->aijk', result, mixing, precision=lax.Precision.HIGHEST)

def advect(state, wind_pair, mixing):
    padded = jnp.pad(state, ((0, 0), (1, 1), (0, 0), (0, 0)))
    return moved(padded, wind_pair, mixing)

def forward(control, winds_full, mixing):
    states = []
    current = jnp.zeros(control.shape[1:], jnp.float32)
    for window in range(SUBW):
        weight_now = SCALE_B if window == 0 else SCALE_Q
        current = advect(current + weight_now * control[window], winds_full[window], mixing)
        states.append(current)
    return jnp.stack(states)

def reference(winds, mixing, innovations, obs_weight, obs_sub, obs_col, obs_count):
    winds_full = untile(winds)
    group_ids = jnp.arange(N_TM, dtype=jnp.int32)[:, None, None, None]
    owner_ids = jnp.arange(N_SPACE, dtype=jnp.int32)[None, None, :, None]
    sub_index = group_ids * SUB_DEV + obs_sub
    lat_index = owner_ids // PXT * TLAT + obs_col // TLON
    lon_index = owner_ids % PXT * TLON + obs_col % TLON
    slot_ids = jnp.arange(PER, dtype=jnp.int32)
    live_slot = slot_ids[None, None, None, :] < obs_count[..., None]
    weights = jnp.where(live_slot[..., None], obs_weight, 0.0)
    state_shape = (SUBW, FIELDS, NLAT, NLON, LEV)

    def spread_profiles(profiles):
        shaped = profiles.reshape(N_TM, N_SPACE, N_SPACE, PER, FIELDS, LEV)
        return jnp.zeros(state_shape, jnp.float32).at[sub_index, :, lat_index, lon_index, :].add(shaped)

    def select_profiles(states):
        return states[sub_index, :, lat_index, lon_index, :].reshape(N_TM, N_SPACE, N_SPACE, PER, PROF)

    def run_model(control):
        return forward(control, winds_full, mixing)
    zero_control = jnp.zeros(state_shape, jnp.float32)
    _, pull_back = jax.vjp(run_model, zero_control)

    def hessian(direction):
        states = run_model(direction)
        return direction + pull_back(spread_profiles(weights * select_profiles(states)))[0]
    gradient = pull_back(spread_profiles(weights * innovations))[0]
    increment = jnp.zeros(state_shape, jnp.float32)
    residual = gradient
    direction = gradient
    norm_now = jnp.sum(residual * residual)
    for step_num in range(ITERS):
        image_vec = hessian(direction)
        step_size = norm_now / jnp.sum(direction * image_vec)
        increment = increment + step_size * direction
        residual = residual - step_size * image_vec
        norm_next = jnp.sum(residual * residual)
        direction = residual + norm_next / norm_now * direction
        norm_now = norm_next
    return (retile(increment), retile(residual))
```

```python
import functools
import jax
import jax.numpy as jnp
from jax import lax
from jax.experimental import pallas as pl
from jax.experimental.pallas import tpu as pltpu
from jax.sharding import PartitionSpec as P

FIELDS = 3
MIXC = 0.25
SCALE_Q = 0.5
PAD = 8
F32 = jnp.float32
BF16 = jnp.bfloat16

VM = pl.BlockSpec(memory_space=pltpu.VMEM)
SM = pl.BlockSpec(memory_space=pltpu.SMEM)


def call(body, ins, specs, outs, vmem=None, flops=1e8, scratch=()):
    nbytes = sum(a.size * a.dtype.itemsize for a in ins)
    nbytes += sum(o.size * o.dtype.itemsize for o in outs)
    return pl.pallas_call(
        body,
        out_shape=outs,
        in_specs=specs,
        out_specs=[VM] * len(outs),
        scratch_shapes=list(scratch),
        compiler_params=pltpu.CompilerParams(vmem_limit_bytes=vmem or 40 * 2**20),
        cost_estimate=pl.CostEstimate(
            flops=int(flops), bytes_accessed=int(nbytes), transcendentals=0
        ),
    )(*ins)


def sds(*shape, dtype=F32):
    return jax.ShapeDtypeStruct(shape, dtype)


def later(x):
    return pltpu.roll(x, 1, 0)


def earlier(x):
    return pltpu.roll(x, x.shape[0] - 1, 0)


def coef(w_ref, i):
    a = w_ref[0, i]
    b = w_ref[1, i]
    ap = jnp.maximum(a, 0.0)
    am = ap - a
    bp = jnp.maximum(b, 0.0)
    bm = bp - b
    return ap, am, bp, bm, 1.0 - (ap + am) - (bp + bm)


def mixed(v, rhs):
    lev = v.shape[1]
    hi = v.astype(BF16)
    lo = (v - hi.astype(F32)).astype(BF16)
    o = jnp.dot(jnp.concatenate([hi, lo], axis=1), rhs, preferred_element_type=F32)
    return v + (o[:, :lev] + o[:, lev:])


def adj_local(w, c):
    ap, am, _, _, c0 = c
    return c0 * w + earlier(ap * w) + later(am * w)


def fwd_local(u, c):
    ap, am, _, _, c0 = c
    return c0 * u + ap * later(u) + am * earlier(u)


def adj_pre(f, rows, w_ref, rhs, mid_ref, ss_ref, sn_ref):
    w = [mixed(x, rhs) for x in rows]
    c = [coef(w_ref, i) for i in range(3)]
    mid_ref[f] = adj_local(w[1], c[1]) + c[2][2] * w[2] + c[0][3] * w[0]
    ss_ref[0, f] = adj_local(w[0], c[0]) + c[1][2] * w[1]
    ss_ref[1, f] = c[0][2] * w[0]
    sn_ref[0, f] = adj_local(w[2], c[2]) + c[1][3] * w[1]
    sn_ref[1, f] = c[2][3] * w[2]


def adj_post(f, mid_ref, ss_ref, sn_ref, rs_ref, rn_ref, fs, fn):
    return [
        (rs_ref[0, f] + ss_ref[1, f]) * fs,
        ss_ref[0, f] + rs_ref[1, f] * fs,
        mid_ref[f],
        sn_ref[0, f] + rn_ref[1, f] * fn,
        (rn_ref[0, f] + sn_ref[1, f]) * fn,
    ]


def adj_second(rows5, w_ref, wh_ref, rhs):
    w = [mixed(x, rhs) for x in rows5]
    c = [coef(w_ref, i) for i in range(3)]
    up = [c[1][2], c[2][2], wh_ref[1]]
    down = [wh_ref[0], c[0][3], c[1][3]]
    return [
        adj_local(w[i + 1], c[i]) + up[i] * w[i + 2] + down[i] * w[i] for i in range(3)
    ]


def fwd_pre(f, u, w_ref, mid_ref, ss_ref, sn_ref):
    c = [coef(w_ref, i) for i in range(3)]
    mid_ref[f] = fwd_local(u[1], c[1]) + c[1][2] * u[0] + c[1][3] * u[2]
    ss_ref[0, f] = u[0]
    ss_ref[1, f] = fwd_local(u[0], c[0]) + c[0][3] * u[1]
    sn_ref[0, f] = u[2]
    sn_ref[1, f] = fwd_local(u[2], c[2]) + c[2][2] * u[1]


def fwd_post(f, mid_ref, ss_ref, sn_ref, rs_ref, rn_ref, w_ref, wh_ref, fs, fn, rhs):
    b0 = w_ref[1, 0]
    b2 = w_ref[1, 2]
    m = [
        rs_ref[1, f] * fs + wh_ref[0] * ss_ref[0, f],
        ss_ref[1, f] + jnp.maximum(b0, 0.0) * (rs_ref[0, f] * fs),
        mid_ref[f],
        sn_ref[1, f] + jnp.maximum(-b2, 0.0) * (rn_ref[0, f] * fn),
        rn_ref[1, f] * fn + wh_ref[1] * sn_ref[0, f],
    ]
    return [mixed(x, rhs) for x in m]


def fwd_second(u5, w_ref, rhs):
    out = []
    for i in range(3):
        c = coef(w_ref, i)
        m = fwd_local(u5[i + 1], c) + c[2] * u5[i] + c[3] * u5[i + 2]
        out.append(mixed(m, rhs))
    return out


def fields(body):
    def step(f, carry):
        body(f)
        return carry

    lax.fori_loop(0, FIELDS, step, 0)


def fold(x):
    own = x[PAD:-PAD]
    return jnp.sum(own.reshape(own.shape[0] // 8, 8, own.shape[1]), axis=0)


def split_store(x, half, c, own_ref, snd_ref, idx):
    n = x.shape[0]
    low = jnp.concatenate([x[n - PAD :], x[: half + PAD]], axis=0)
    high = jnp.concatenate([x[half - PAD :], x[:PAD]], axis=0)

    @pl.when(c == 0)
    def _():
        own_ref[idx] = low
        snd_ref[idx] = high

    @pl.when(c != 0)
    def _():
        own_ref[idx] = high
        snd_ref[idx] = low


def pack_body(w_ref, d_ref, i_ref, o_ref):
    lev = o_ref.shape[-1]
    live = i_ref[...] >= 0.0
    for f in range(FIELDS):
        w = jnp.where(live, w_ref[:, :, f * lev : (f + 1) * lev], 0.0)
        o_ref[:, f] = w
        o_ref[:, FIELDS + f] = w * d_ref[:, :, f * lev : (f + 1) * lev]
    o_ref[:, 2 * FIELDS] = i_ref[...]


def scatter_body(half, c_ref, idx_ref, p_ref, do_ref, ds_ref, go_ref, gs_ref, acc):
    owners, slots = idx_ref.shape
    blocks = 2 * FIELDS + 1
    lev = p_ref.shape[1]
    cells = acc.shape[0] // 8
    cols = 2 * half
    c = c_ref[0]
    chunk = 64

    def clear(t, carry):
        acc[pl.ds(pl.multiple_of(t * (8 * chunk), 8 * chunk), 8 * chunk), :] = jnp.zeros(
            (8 * chunk, lev), F32
        )
        return carry

    lax.fori_loop(0, cells // chunk, clear, 0)

    def put(o, carry):
        for s in range(slots):
            row = pl.multiple_of(idx_ref[o, s] * 8, 8)
            x = p_ref[pl.ds(o * (blocks * slots) + s, blocks, stride=slots), :]
            acc[pl.ds(row, blocks), :] += x
        return carry

    lax.fori_loop(0, owners, put, 0)

    for w in range(2):

        def one(i, carry):
            base = (w * 3 + i) * (cols * 8)
            for f in range(FIELDS):
                x = acc[pl.ds(base + f, cols, stride=8), :]
                split_store(x, half, c, do_ref, ds_ref, (w, f, i))
                y = acc[pl.ds(base + FIELDS + f, cols, stride=8), :]
                split_store(y, half, c, go_ref, gs_ref, (w, f, i))
            return carry

        lax.fori_loop(0, 3, one, 0)


def wind_body(half, c_ref, w_ref, m_ref, o_ref, s_ref, ra_ref, rf_ref):
    c = c_ref[0]
    for w in range(2):

        def one(i, carry):
            for k in range(2):
                split_store(w_ref[w, k, i].astype(F32), half, c, o_ref, s_ref, (w, k, i))
            return carry

        lax.fori_loop(0, 3, one, 0)
    for m, ref in ((m_ref[...] * MIXC, ra_ref), (m_ref[...].T * MIXC, rf_ref)):
        hi = m.astype(BF16)
        lo = (m - hi.astype(F32)).astype(BF16)
        line = jnp.concatenate([hi, lo], axis=1)
        ref[...] = jnp.concatenate([line, line], axis=0)


def turn_first_body(g3_ref, g2_ref, w3_ref, ra_ref, mid_ref, ss_ref, sn_ref):
    rhs = ra_ref[...]

    def one(f):
        adj_pre(f, [g3_ref[f, i] for i in range(3)], w3_ref, rhs, mid_ref, ss_ref, sn_ref)
        ss_ref[2, f] = g2_ref[f, 0]
        sn_ref[2, f] = g2_ref[f, 2]

    fields(one)


def five(f, f_ref, rs_ref, rn_ref, ext):
    if ext:
        return [rs_ref[2, f]] + [f_ref[f, i] for i in range(3)] + [rn_ref[2, f]]
    return [f_ref[f, i] for i in range(5)]


def adj_mid_body(ext, *refs):
    (fl, mid, ss, sn, rs, rn, f2, f1, w2, wh2, w1, ra) = refs[:12]
    n = 12
    if ext:
        g0 = refs[n]
        n += 1
    g3, g2, mid_o, ss_o, sn_o = refs[n:]
    fs, fn = fl[0], fl[1]
    rhs = ra[...]

    def one(f):
        lam = adj_post(f, mid, ss, sn, rs, rn, fs, fn)
        for i in range(5):
            g3[f, i] = lam[i] * SCALE_Q
        src = five(f, f2, rs, rn, ext)
        out = adj_second([lam[i] + src[i] for i in range(5)], w2, wh2, rhs)
        for i in range(3):
            g2[f, i] = out[i] * SCALE_Q
        adj_pre(f, [out[i] + f1[f, i] for i in range(3)], w1, rhs, mid_o, ss_o, sn_o)
        if ext:
            ss_o[2, f] = g0[f, 0]
            sn_o[2, f] = g0[f, 2]

    fields(one)


def adj_last_body(mode, *refs):
    ext = mode == 0
    (fl, mid, ss, sn, rs, rn, f0, w0, wh0, ra) = refs[:10]
    n = 10
    if mode == 1:
        sc, g0, g1 = refs[n : n + 3]
        n += 3
    outs = refs[n:]
    fs, fn = fl[0], fl[1]
    rhs = ra[...]

    def one(f):
        lam = adj_post(f, mid, ss, sn, rs, rn, fs, fn)
        src = five(f, f0, rs, rn, ext)
        out = adj_second([lam[i] + src[i] for i in range(5)], w0, wh0, rhs)
        one_half = [x * SCALE_Q for x in lam]
        if mode == 1:
            a = sc[0]
            one_half = [(1.0 - a) * g1[f, i] - a * one_half[i] for i in range(5)]
            out = [(1.0 - a) * g0[f, i] - a * out[i] for i in range(3)]
        for i in range(5):
            outs[1][f, i] = one_half[i]
        for i in range(3):
            outs[0][f, i] = out[i]
        if mode < 2:
            fwd_pre(f, out, w0, *outs[2:5])

    fields(one)


def fwd_first_body(fl, mid, ss, sn, rs, rn, v1, v2, w0, wh0, w1, w2, rf, *outs):
    x0, x1, mid_o, ss_o, sn_o = outs
    fs, fn = fl[0], fl[1]
    rhs = rf[...]

    def one(f):
        x5 = fwd_post(f, mid, ss, sn, rs, rn, w0, wh0, fs, fn, rhs)
        for i in range(5):
            x0[f, i] = x5[i]
        x3 = fwd_second([x5[i] + SCALE_Q * v1[f, i] for i in range(5)], w1, rhs)
        for i in range(3):
            x1[f, i] = x3[i]
        fwd_pre(f, [x3[i] + SCALE_Q * v2[f, i] for i in range(3)], w2, mid_o, ss_o, sn_o)

    fields(one)


def edge(x, half):
    return jnp.concatenate([x[half : half + PAD], x[PAD : 2 * PAD]], axis=0)


def fwd_last_body(half, fl, mid, ss, sn, rs, rn, v3, x0, x1, w2, wh2, w3, rf, *outs):
    x2, x3, eg = outs
    fs, fn = fl[0], fl[1]
    rhs = rf[...]

    def one(f):
        x5 = fwd_post(f, mid, ss, sn, rs, rn, w2, wh2, fs, fn, rhs)
        for i in range(5):
            x2[f, i] = x5[i]
            eg[f, 8 + i] = edge(x5[i], half)
            eg[f, i] = edge(x0[f, i], half)
        y3 = fwd_second([x5[i] + SCALE_Q * v3[f, i] for i in range(5)], w3, rhs)
        for i in range(3):
            x3[f, i] = y3[i]
            eg[f, 13 + i] = edge(y3[i], half)
            eg[f, 5 + i] = edge(x1[f, i], half)

    fields(one)


def fixed(x, e):
    return jnp.concatenate([e[:PAD], x[PAD:-PAD], e[PAD:]], axis=0)


def turn_body(second, *refs):
    x3, eg, d3, w3, ra = refs[:5]
    n = 5
    if second:
        sc, old = refs[n : n + 2]
        n += 2
    y3, mid, ss, sn, q = refs[n:]
    rhs = ra[...]
    q[...] = jnp.zeros_like(q)

    def one(f):
        rows = []
        for i in range(3):
            y = fixed(x3[f, i], eg[f, 13 + i])
            if second:
                y = y + sc[0] * old[f, i]
            y3[f, i] = y
            t = d3[f, i] * y
            q[...] += fold(t * y)
            rows.append(t)
        adj_pre(f, rows, w3, rhs, mid, ss, sn)

    fields(one)


def rest_body(second, *refs):
    x0, x1, x2, eg, d0, d1, d2, ds, dn = refs[:9]
    n = 9
    if second:
        sc, old0, old1, old2 = refs[n : n + 4]
        n += 4
    else:
        old0 = old1 = old2 = None
    y0, y1, y2, f0, f1, f2, q = refs[n:]
    q[...] = jnp.zeros_like(q)

    def one(f):
        for x, rows, at, d, w, old, y_o, f_o in (
            (x0, 5, 0, d0, 0, old0, y0, f0),
            (x1, 3, 5, d1, None, old1, y1, f1),
            (x2, 5, 8, d2, 1, old2, y2, f2),
        ):
            for i in range(rows):
                y = fixed(x[f, i], eg[f, at + i])
                if second:
                    y = y + sc[0] * old[f, i]
                y_o[f, i] = y
                if rows == 3:
                    t = d[f, i] * y
                    q[...] += fold(t * y)
                elif i == 0:
                    t = ds[w, f] * y
                elif i == 4:
                    t = dn[w, f] * y
                else:
                    t = d[f, i - 1] * y
                    q[...] += fold(t * y)
                f_o[f, i] = t

    fields(one)


def norm_body(v0, v1, v2, v3, q):
    q[...] = jnp.zeros_like(q)

    def one(f):
        for v, off in ((v0, 0), (v1, 1), (v2, 0), (v3, 1)):
            for i in range(3):
                x = v[f, i + off]
                q[...] += fold(x * x)

    fields(one)


def resid_body(sc, v0, v1, g0, g1, g2, g3, z2, z3, r2, r3, q):
    a = sc[0]
    q[...] = jnp.zeros_like(q)

    def dots(r, g):
        q[0] += fold(r * r)
        q[1] += fold(r * g)

    def one(f):
        for i in range(5):
            r = (1.0 - a) * g3[f, i] - a * z3[f, i]
            r3[f, i] = r
            if 0 < i < 4:
                dots(r, g3[f, i])
                dots(v1[f, i], g1[f, i])
        for i in range(3):
            r = (1.0 - a) * g2[f, i] - a * z2[f, i]
            r2[f, i] = r
            dots(r, g2[f, i])
            dots(v0[f, i], g0[f, i])

    fields(one)


def final_body(kind, c_ref, sc, *refs):
    r = refs[0:4]
    g = refs[4:8]
    n = 8
    if kind == "res":
        z = refs[8:12]
        n = 12
    keep, send = refs[n:]
    c = c_ref[0]
    beta, a0, a1 = sc[0], sc[1], sc[2]

    def one(f):
        for k in range(4):
            off = k % 2
            for i in range(3):
                res = r[k][f, i + off][PAD:-PAD]
                grad = g[k][f, i + off][PAD:-PAD]
                d = res + beta * grad
                if kind == "res":
                    val = res - a1 * (d + z[k][f, i + off][PAD:-PAD])
                else:
                    val = a0 * grad + a1 * d

                @pl.when(c == k // 2)
                def _():
                    keep[k % 2, f, i] = val

                @pl.when(c != k // 2)
                def _():
                    send[k % 2, f, i] = val

    fields(one)


def per_device(winds, mixing, innovations, obs_weight, obs_sub, obs_col, obs_count):
    owners, slots = obs_sub.shape[2], obs_sub.shape[3]
    lev = mixing.shape[0]
    cols = winds.shape[4]
    half = cols // 2
    wide = half + 2 * PAD
    cells = winds.shape[3] * cols
    c = lax.axis_index("tm").astype(jnp.int32)
    pos = lax.axis_index("space")
    bands = lax.axis_size("space")
    c_arr = c.reshape(1)
    flags = jnp.stack([(pos > 0), (pos < bands - 1)]).astype(F32)
    north = [(i, (i + 1) % bands) for i in range(bands)]
    south = [((i + 1) % bands, i) for i in range(bands)]

    def swap(x):
        return lax.ppermute(x, "tm", [(0, 1), (1, 0)])

    def exchange(ss, sn):
        return lax.ppermute(sn, "space", north), lax.ppermute(ss, "space", south)

    def total(parts):
        vals = jnp.stack([jnp.sum(p) for p in parts])
        vals = vals + swap(vals)
        msg = jnp.broadcast_to(
            jnp.pad(vals, (0, lev - len(parts)))[None, None, :], (bands, 1, lev)
        )
        got = lax.all_to_all(msg, "space", split_axis=0, concat_axis=0, tiled=True)
        return jnp.sum(got, axis=(0, 1))

    live = (
        jnp.arange(slots, dtype=jnp.int32)[None, :] < obs_count.reshape(owners)[:, None]
    )
    place = (obs_sub * cells + obs_col).reshape(owners, slots)
    place = jnp.where(live, place, -1).astype(F32)
    place = jnp.broadcast_to(place[..., None], (owners, slots, lev))
    blocks = 2 * FIELDS + 1
    packed = call(
        pack_body,
        (
            obs_weight.reshape(owners, slots, -1),
            innovations.reshape(owners, slots, -1),
            place,
        ),
        [VM] * 3,
        [sds(owners, blocks, slots, lev)],
    )[0]
    got = lax.all_to_all(packed, "space", split_axis=0, concat_axis=0, tiled=True)

    w_own, w_snd, ra, rf = call(
        functools.partial(wind_body, half),
        (c_arr, winds[:, 0], mixing),
        [SM, VM, VM],
        [sds(2, 2, 3, wide, lev)] * 2 + [sds(2 * lev, 2 * lev, dtype=BF16)] * 2,
    )
    w_got = swap(w_snd)
    first = c == 0
    w01 = jnp.where(first, w_own, w_got)
    w23 = jnp.where(first, w_got, w_own)
    w0, w1, w2, w3 = w01[0], w01[1], w23[0], w23[1]
    up = jnp.stack([jnp.maximum(-w0[1, 2], 0.0), jnp.maximum(-w2[1, 2], 0.0)])
    down = jnp.stack([jnp.maximum(w0[1, 0], 0.0), jnp.maximum(w2[1, 0], 0.0)])
    from_s, from_n = exchange(down, up)
    from_s = jnp.where(pos > 0, from_s, 0.0)
    from_n = jnp.where(pos < bands - 1, from_n, 0.0)
    wh0 = jnp.stack([from_s[0], from_n[0]])
    wh2 = jnp.stack([from_s[1], from_n[1]])

    idx = jnp.maximum(got[:, 2 * FIELDS, :, 0], 0.0).astype(jnp.int32)
    d_own, d_snd, g_own, g_snd = call(
        functools.partial(scatter_body, half),
        (c_arr, idx, got.reshape(owners * blocks * slots, lev)),
        [SM, SM, VM],
        [sds(2, FIELDS, 3, wide, lev)] * 4,
        scratch=[pltpu.VMEM((2 * cells * 8, lev), F32)],
    )
    g_got = swap(g_snd)
    f01 = jnp.where(first, g_own, g_got)
    f23 = jnp.where(first, g_got, g_own)
    d_got = swap(d_snd)
    d01 = jnp.where(first, d_own, d_got)
    d23 = jnp.where(first, d_got, d_own)
    dd0, dd1, dd2, dd3 = d01[0], d01[1], d23[0], d23[1]
    ds, dn = exchange(
        jnp.stack([dd0[:, 0], dd2[:, 0]]), jnp.stack([dd0[:, 2], dd2[:, 2]])
    )

    row3 = sds(FIELDS, 3, wide, lev)
    row5 = sds(FIELDS, 5, wide, lev)
    mid_t = sds(FIELDS, wide, lev)

    def msg(n):
        return sds(n, FIELDS, wide, lev)

    part = sds(8, lev)

    def adj_mid(state, f2, f1, g0=None):
        mid, ss, sn = state
        rs, rn = exchange(ss, sn)
        ext = g0 is not None
        n = 3 if ext else 2
        ins = (flags, mid, ss, sn, rs, rn, f2, f1, w2, wh2, w1, ra) + ((g0,) if ext else ())
        o = call(
            functools.partial(adj_mid_body, ext),
            ins,
            [SM] + [VM] * (len(ins) - 1),
            [row5, row3, mid_t, msg(n), msg(n)],
        )
        return o[0], o[1], tuple(o[2:])

    def adj_last(mode, state, f0, extra=()):
        mid, ss, sn = state
        rs, rn = exchange(ss, sn)
        ins = (flags, mid, ss, sn, rs, rn, f0, w0, wh0, ra) + extra
        specs = [SM] + [VM] * 9 + ([SM, VM, VM] if extra else [])
        outs = [row3, row5] + ([mid_t, msg(2), msg(2)] if mode < 2 else [])
        o = call(functools.partial(adj_last_body, mode), ins, specs, outs)
        return o[0], o[1], tuple(o[2:])

    def fwd_first(state, v1, v2):
        mid, ss, sn = state
        rs, rn = exchange(ss, sn)
        ins = (flags, mid, ss, sn, rs, rn, v1, v2, w0, wh0, w1, w2, rf)
        o = call(
            fwd_first_body, ins, [SM] + [VM] * 12, [row5, row3, mid_t, msg(2), msg(2)]
        )
        return o[0], o[1], tuple(o[2:])

    def fwd_last(state, v3, x0, x1):
        mid, ss, sn = state
        rs, rn = exchange(ss, sn)
        ins = (flags, mid, ss, sn, rs, rn, v3, x0, x1, w2, wh2, w3, rf)
        return call(
            functools.partial(fwd_last_body, half),
            ins,
            [SM] + [VM] * 12,
            [row5, row3, sds(FIELDS, 16, 2 * PAD, lev)],
        )

    def turn(xs, eg, beta=None, old=None):
        eg = swap(eg)
        second = beta is not None
        x0, x1, x2, x3 = xs
        ex = (beta, old[3]) if second else ()
        o = call(
            functools.partial(turn_body, second),
            (x3, eg, dd3, w3, ra) + ex,
            [VM] * 5 + ([SM, VM] if second else []),
            [row3, mid_t, msg(2), msg(2), part],
        )
        y3, state, q3 = o[0], tuple(o[1:4]), o[4]
        ex = (beta,) + old[:3] if second else ()
        y0, y1, y2, f0, f1, f2, q = call(
            functools.partial(rest_body, second),
            (x0, x1, x2, eg, dd0, dd1, dd2, ds, dn) + ex,
            [VM] * 9 + ([SM] + [VM] * 3 if second else []),
            [row5, row3, row5, row5, row3, row5, part],
        )
        return state, (y0, y1, y2, y3), (f0, f1, f2), q3 + q

    o = call(
        turn_first_body,
        (f23[1], f23[0], w3, ra),
        [VM] * 4,
        [mid_t, msg(3), msg(3)],
    )
    g3, g2, state = adj_mid(tuple(o), f23[0], f01[1], f01[0])
    g0, g1, state = adj_last(0, state, f01[0])
    rr_part = call(norm_body, (g0, g1, g2, g3), [VM] * 4, [part])[0]

    x0, x1, state = fwd_first(state, g1, g2)
    x2, x3, eg = fwd_last(state, g3, x0, x1)
    state, ys, fs, q = turn((x0, x1, x2, x3), eg)
    sums = total([rr_part, q])
    rr0 = sums[0]
    a0 = rr0 / (rr0 + sums[1])
    z3, z2, state = adj_mid(state, fs[2], fs[1])
    a0_arr = a0.reshape(1)
    v0, v1, state = adj_last(1, state, fs[0], (a0_arr, g0, g1))
    v2, v3, q = call(
        resid_body,
        (a0_arr, v0, v1, g0, g1, g2, g3, z2, z3),
        [SM] + [VM] * 8,
        [row3, row5, sds(2, 8, lev)],
    )
    sums = total([q[0], q[1]])
    rr1 = sums[0]
    beta = rr1 / rr0
    dd = rr1 + beta * (2.0 * sums[1] + beta * rr0)

    x0, x1, state = fwd_first(state, v1, v2)
    x2, x3, eg = fwd_last(state, v3, x0, x1)
    state, _, fs, q = turn((x0, x1, x2, x3), eg, beta.reshape(1), ys)
    a1 = rr1 / (dd + total([q])[0])
    scal = jnp.stack([beta, a0, a1])
    z3, z2, state = adj_mid(state, fs[2], fs[1])
    z0, z1, _ = adj_last(2, state, fs[0])

    shape = sds(2, FIELDS, 3, half, lev)
    keep_i, send_i = call(
        functools.partial(final_body, "inc"),
        (c_arr, scal, v0, v1, v2, v3, g0, g1, g2, g3),
        [SM, SM] + [VM] * 8,
        [shape, shape],
    )
    keep_r, send_r = call(
        functools.partial(final_body, "res"),
        (c_arr, scal, v0, v1, v2, v3, g0, g1, g2, g3, z0, z1, z2, z3),
        [SM, SM] + [VM] * 12,
        [shape, shape],
    )

    def whole(keep, send):
        other = swap(send)
        return jnp.where(
            first,
            jnp.concatenate([keep, other], axis=3),
            jnp.concatenate([other, keep], axis=3),
        )[:, None]

    return whole(keep_i, send_i), whole(keep_r, send_r)


def solution(mesh):
    in_specs = (
        P("tm", "space", None, None, None, None),
        P(),
        P("tm", "space", None, None, None),
        P("tm", "space", None, None, None),
        P("tm", "space", None, None),
        P("tm", "space", None, None),
        P("tm", "space", None),
    )
    out_specs = (P("tm", "space", None, None, None, None), P("tm", "space", None, None, None, None))
    return jax.shard_map(
        per_device, mesh=mesh, in_specs=in_specs, out_specs=out_specs, check_vma=False
    )
```

```python
import functools
import jax
import jax.numpy as jnp
from jax import lax
from jax.experimental import pallas as pl
from jax.experimental.pallas import tpu as pltpu
from jax.sharding import PartitionSpec as P

FIELDS = 3
MIXC = 0.25
SCALE_Q = 0.5
GROUPS = (3,)
PAD = 8
F32 = jnp.float32
BF16 = jnp.bfloat16

VM = pl.BlockSpec(memory_space=pltpu.VMEM)
SM = pl.BlockSpec(memory_space=pltpu.SMEM)


def call(body, ins, specs, outs, vmem=None, flops=1e8, scratch=(), out_specs=None):
    nbytes = sum(a.size * a.dtype.itemsize for a in ins)
    nbytes += sum(o.size * o.dtype.itemsize for o in outs)
    return pl.pallas_call(
        body,
        out_shape=outs,
        in_specs=specs,
        out_specs=out_specs or [VM] * len(outs),
        scratch_shapes=list(scratch),
        compiler_params=pltpu.CompilerParams(vmem_limit_bytes=vmem or 6 * 2**20),
        cost_estimate=pl.CostEstimate(
            flops=int(flops), bytes_accessed=int(nbytes), transcendentals=0
        ),
    )(*ins)


def sds(*shape, dtype=F32):
    return jax.ShapeDtypeStruct(shape, dtype)


def later(x):
    return pltpu.roll(x, 1, 0)


def earlier(x):
    return pltpu.roll(x, x.shape[0] - 1, 0)


def coef(w_ref, i):
    a = w_ref[0, i]
    b = w_ref[1, i]
    ap = jnp.maximum(a, 0.0)
    am = ap - a
    bp = jnp.maximum(b, 0.0)
    bm = bp - b
    return ap, am, bp, bm, 1.0 - (ap + am) - (bp + bm)


def mixed(v, rhs):
    lev = v.shape[1]
    hi = v.astype(BF16)
    lo = (v - hi.astype(F32)).astype(BF16)
    o = jnp.dot(jnp.concatenate([hi, lo], axis=1), rhs, preferred_element_type=F32)
    return v + (o[:, :lev] + o[:, lev:])


def adj_local(w, c):
    ap, am, _, _, c0 = c
    return c0 * w + earlier(ap * w) + later(am * w)


def fwd_local(u, c):
    ap, am, _, _, c0 = c
    return c0 * u + ap * later(u) + am * earlier(u)


def adj_pre(f, rows, w_ref, rhs, mid_ref, ss_ref, sn_ref):
    w = [mixed(x, rhs) for x in rows]
    c = [coef(w_ref, i) for i in range(3)]
    mid_ref[f] = adj_local(w[1], c[1]) + c[2][2] * w[2] + c[0][3] * w[0]
    ss_ref[0, f] = adj_local(w[0], c[0]) + c[1][2] * w[1]
    ss_ref[1, f] = c[0][2] * w[0]
    sn_ref[0, f] = adj_local(w[2], c[2]) + c[1][3] * w[1]
    sn_ref[1, f] = c[2][3] * w[2]


def adj_post(f, mid_ref, ss_ref, sn_ref, rs_ref, rn_ref, fs, fn):
    return [
        (rs_ref[0, f] + ss_ref[1, f]) * fs,
        ss_ref[0, f] + rs_ref[1, f] * fs,
        mid_ref[f],
        sn_ref[0, f] + rn_ref[1, f] * fn,
        (rn_ref[0, f] + sn_ref[1, f]) * fn,
    ]


def adj_second(rows5, w_ref, wh_ref, rhs):
    w = [mixed(x, rhs) for x in rows5]
    c = [coef(w_ref, i) for i in range(3)]
    up = [c[1][2], c[2][2], wh_ref[1]]
    down = [wh_ref[0], c[0][3], c[1][3]]
    return [
        adj_local(w[i + 1], c[i]) + up[i] * w[i + 2] + down[i] * w[i] for i in range(3)
    ]


def fwd_pre(f, u, w_ref, mid_ref, ss_ref, sn_ref):
    c = [coef(w_ref, i) for i in range(3)]
    mid_ref[f] = fwd_local(u[1], c[1]) + c[1][2] * u[0] + c[1][3] * u[2]
    ss_ref[0, f] = u[0]
    ss_ref[1, f] = fwd_local(u[0], c[0]) + c[0][3] * u[1]
    sn_ref[0, f] = u[2]
    sn_ref[1, f] = fwd_local(u[2], c[2]) + c[2][2] * u[1]


def fwd_post(f, mid_ref, ss_ref, sn_ref, rs_ref, rn_ref, w_ref, wh_ref, fs, fn, rhs):
    b0 = w_ref[1, 0]
    b2 = w_ref[1, 2]
    m = [
        rs_ref[1, f] * fs + wh_ref[0] * ss_ref[0, f],
        ss_ref[1, f] + jnp.maximum(b0, 0.0) * (rs_ref[0, f] * fs),
        mid_ref[f],
        sn_ref[1, f] + jnp.maximum(-b2, 0.0) * (rn_ref[0, f] * fn),
        rn_ref[1, f] * fn + wh_ref[1] * sn_ref[0, f],
    ]
    return [mixed(x, rhs) for x in m]


def fwd_second(u5, w_ref, rhs):
    out = []
    for i in range(3):
        c = coef(w_ref, i)
        m = fwd_local(u5[i + 1], c) + c[2] * u5[i] + c[3] * u5[i + 2]
        out.append(mixed(m, rhs))
    return out


def fields(n, body):
    if n == 1:
        body(0)
        return

    def step(f, carry):
        body(f)
        return carry

    lax.fori_loop(0, n, step, 0)


def tot(s_ref, i):
    return jnp.sum(s_ref[i], keepdims=True)


def first_step(s_ref):
    rr = tot(s_ref, 0)
    return rr / (rr + tot(s_ref, 1))


def fold(x):
    own = x[PAD:-PAD]
    return jnp.sum(own.reshape(own.shape[0] // 8, 8, own.shape[1]), axis=0)


def split_store(x, half, c, own_ref, snd_ref, idx):
    n = x.shape[0]
    low = jnp.concatenate([x[n - PAD :], x[: half + PAD]], axis=0)
    high = jnp.concatenate([x[half - PAD :], x[:PAD]], axis=0)

    @pl.when(c == 0)
    def _():
        own_ref[idx] = low
        snd_ref[idx] = high

    @pl.when(c != 0)
    def _():
        own_ref[idx] = high
        snd_ref[idx] = low


def pack_body(w_ref, d_ref, i_ref, o_ref):
    lev = o_ref.shape[-1]
    live = i_ref[...] >= 0.0
    for f in range(FIELDS):
        w = jnp.where(live, w_ref[:, :, f * lev : (f + 1) * lev], 0.0)
        o_ref[:, f] = w
        o_ref[:, FIELDS + f] = w * d_ref[:, :, f * lev : (f + 1) * lev]
    o_ref[:, 2 * FIELDS] = i_ref[...]


def scatter_body(half, c_ref, idx_ref, p_ref, do_ref, ds_ref, go_ref, gs_ref, acc):
    owners, slots = idx_ref.shape
    blocks = 2 * FIELDS + 1
    lev = p_ref.shape[1]
    cells = acc.shape[0] // 8
    cols = 2 * half
    c = c_ref[0]
    chunk = 64

    def clear(t, carry):
        acc[pl.ds(pl.multiple_of(t * (8 * chunk), 8 * chunk), 8 * chunk), :] = jnp.zeros(
            (8 * chunk, lev), F32
        )
        return carry

    lax.fori_loop(0, cells // chunk, clear, 0)

    def put(o, carry):
        for s in range(slots):
            row = pl.multiple_of(idx_ref[o, s] * 8, 8)
            x = p_ref[pl.ds(o * (blocks * slots) + s, blocks, stride=slots), :]
            acc[pl.ds(row, blocks), :] += x
        return carry

    lax.fori_loop(0, owners, put, 0)

    for w in range(2):

        def one(i, carry):
            base = (w * 3 + i) * (cols * 8)
            for f in range(FIELDS):
                x = acc[pl.ds(base + f, cols, stride=8), :]
                split_store(x, half, c, do_ref, ds_ref, (w, f, i))
                y = acc[pl.ds(base + FIELDS + f, cols, stride=8), :]
                split_store(y, half, c, go_ref, gs_ref, (w, f, i))
            return carry

        lax.fori_loop(0, 3, one, 0)


def wind_body(half, c_ref, w_ref, m_ref, o_ref, s_ref, ra_ref, rf_ref):
    c = c_ref[0]
    for w in range(2):

        def one(i, carry):
            for k in range(2):
                split_store(w_ref[w, k, i].astype(F32), half, c, o_ref, s_ref, (w, k, i))
            return carry

        lax.fori_loop(0, 3, one, 0)
    for m, ref in ((m_ref[...] * MIXC, ra_ref), (m_ref[...].T * MIXC, rf_ref)):
        hi = m.astype(BF16)
        lo = (m - hi.astype(F32)).astype(BF16)
        line = jnp.concatenate([hi, lo], axis=1)
        ref[...] = jnp.concatenate([line, line], axis=0)


def pick_body(f0, c_ref, own_ref, got_ref, *outs):
    c = c_ref[0]
    nf = outs[0].shape[0]

    def put(src, dst):
        for w in range(2):
            for f in range(nf):
                dst[w][f] = src[w, f0 + f]

    @pl.when(c == 0)
    def _():
        put(own_ref, outs[:2])
        put(got_ref, outs[2:4])

    @pl.when(c != 0)
    def _():
        put(got_ref, outs[:2])
        put(own_ref, outs[2:4])


def pick_wind_body(c_ref, own_ref, got_ref, w0, w1, w2, w3, ss, sn):
    pick_body(0, c_ref, own_ref, got_ref, w0, w1, w2, w3)
    for k, w in enumerate((w0, w2)):
        ss[k] = jnp.maximum(w[1, 0], 0.0)
        sn[k] = jnp.maximum(-w[1, 2], 0.0)


def turn_first_body(g3_ref, g2_ref, w3_ref, ra_ref, mid_ref, ss_ref, sn_ref):
    rhs = ra_ref[...]

    def one(f):
        adj_pre(f, [g3_ref[f, i] for i in range(3)], w3_ref, rhs, mid_ref, ss_ref, sn_ref)
        ss_ref[2, f] = g2_ref[f, 0]
        sn_ref[2, f] = g2_ref[f, 2]

    fields(g3_ref.shape[0], one)


def five(f, f_ref, rs_ref, rn_ref, ext):
    if ext:
        return [rs_ref[2, f]] + [f_ref[f, i] for i in range(3)] + [rn_ref[2, f]]
    return [f_ref[f, i] for i in range(5)]


def adj_mid_body(ext, *refs):
    (fl, mid, ss, sn, rs, rn, f2, f1, w2, wh2, w1, ra) = refs[:12]
    n = 12
    if ext:
        g0 = refs[n]
        n += 1
    g3, g2, mid_o, ss_o, sn_o = refs[n:]
    fs, fn = fl[0], fl[1]
    rhs = ra[...]

    def one(f):
        lam = adj_post(f, mid, ss, sn, rs, rn, fs, fn)
        for i in range(5):
            g3[f, i] = lam[i] * SCALE_Q
        src = five(f, f2, rs, rn, ext)
        out = adj_second([lam[i] + src[i] for i in range(5)], w2, wh2, rhs)
        for i in range(3):
            g2[f, i] = out[i] * SCALE_Q
        adj_pre(f, [out[i] + f1[f, i] for i in range(3)], w1, rhs, mid_o, ss_o, sn_o)
        if ext:
            ss_o[2, f] = g0[f, 0]
            sn_o[2, f] = g0[f, 2]

    fields(mid.shape[0], one)


def adj_last_body(mode, *refs):
    ext = mode == 0
    (fl, mid, ss, sn, rs, rn, f0, w0, wh0, ra) = refs[:10]
    n = 10
    if mode == 1:
        sc, g0, g1 = refs[n : n + 3]
        n += 3
    outs = refs[n:]
    fs, fn = fl[0], fl[1]
    rhs = ra[...]
    if mode == 1:
        a = first_step(sc)

    def one(f):
        lam = adj_post(f, mid, ss, sn, rs, rn, fs, fn)
        src = five(f, f0, rs, rn, ext)
        out = adj_second([lam[i] + src[i] for i in range(5)], w0, wh0, rhs)
        one_half = [x * SCALE_Q for x in lam]
        if mode == 1:
            one_half = [(1.0 - a) * g1[f, i] - a * one_half[i] for i in range(5)]
            out = [(1.0 - a) * g0[f, i] - a * out[i] for i in range(3)]
        for i in range(5):
            outs[1][f, i] = one_half[i]
        for i in range(3):
            outs[0][f, i] = out[i]
        if mode < 2:
            fwd_pre(f, out, w0, *outs[2:5])

    fields(mid.shape[0], one)


def fwd_first_body(fl, mid, ss, sn, rs, rn, v1, v2, w0, wh0, w1, w2, rf, *outs):
    x0, x1, mid_o, ss_o, sn_o = outs
    fs, fn = fl[0], fl[1]
    rhs = rf[...]

    def one(f):
        x5 = fwd_post(f, mid, ss, sn, rs, rn, w0, wh0, fs, fn, rhs)
        for i in range(5):
            x0[f, i] = x5[i]
        x3 = fwd_second([x5[i] + SCALE_Q * v1[f, i] for i in range(5)], w1, rhs)
        for i in range(3):
            x1[f, i] = x3[i]
        fwd_pre(f, [x3[i] + SCALE_Q * v2[f, i] for i in range(3)], w2, mid_o, ss_o, sn_o)

    fields(mid.shape[0], one)


def edge(x, half):
    return jnp.concatenate([x[half : half + PAD], x[PAD : 2 * PAD]], axis=0)


def fwd_last_body(half, fl, mid, ss, sn, rs, rn, v3, x0, x1, w2, wh2, w3, rf, *outs):
    x2, x3, eg = outs
    fs, fn = fl[0], fl[1]
    rhs = rf[...]

    def one(f):
        x5 = fwd_post(f, mid, ss, sn, rs, rn, w2, wh2, fs, fn, rhs)
        for i in range(5):
            x2[f, i] = x5[i]
            eg[f, 8 + i] = edge(x5[i], half)
            eg[f, i] = edge(x0[f, i], half)
        y3 = fwd_second([x5[i] + SCALE_Q * v3[f, i] for i in range(5)], w3, rhs)
        for i in range(3):
            x3[f, i] = y3[i]
            eg[f, 13 + i] = edge(y3[i], half)
            eg[f, 5 + i] = edge(x1[f, i], half)

    fields(mid.shape[0], one)


def fixed(x, e):
    return jnp.concatenate([e[:PAD], x[PAD:-PAD], e[PAD:]], axis=0)


def turn_body(second, *refs):
    x3, eg, d3, w3, ra = refs[:5]
    n = 5
    if second:
        s1, s2, old = refs[n : n + 3]
        n += 3
        beta = tot(s2, 0) / tot(s1, 0)
    y3, mid, ss, sn, q = refs[n:]
    rhs = ra[...]
    q[...] = jnp.zeros_like(q)

    def one(f):
        rows = []
        for i in range(3):
            y = fixed(x3[f, i], eg[f, 13 + i])
            if second:
                y = y + beta * old[f, i]
            y3[f, i] = y
            t = d3[f, i] * y
            q[...] += fold(t * y)
            rows.append(t)
        adj_pre(f, rows, w3, rhs, mid, ss, sn)

    fields(x3.shape[0], one)


def rest_body(second, *refs):
    x0, x1, x2, eg, d0, d1, d2, ds, dn = refs[:9]
    n = 9
    if second:
        s1, s2, old0, old1, old2 = refs[n : n + 5]
        n += 5
        beta = tot(s2, 0) / tot(s1, 0)
    else:
        old0 = old1 = old2 = None
    y0, y1, y2, f0, f1, f2, q = refs[n:]
    q[...] = jnp.zeros_like(q)

    def one(f):
        for x, rows, at, d, w, old, y_o, f_o in (
            (x0, 5, 0, d0, 0, old0, y0, f0),
            (x1, 3, 5, d1, None, old1, y1, f1),
            (x2, 5, 8, d2, 1, old2, y2, f2),
        ):
            for i in range(rows):
                y = fixed(x[f, i], eg[f, at + i])
                if second:
                    y = y + beta * old[f, i]
                y_o[f, i] = y
                if rows == 3:
                    t = d[f, i] * y
                    q[...] += fold(t * y)
                elif i == 0:
                    t = ds[w, f] * y
                elif i == 4:
                    t = dn[w, f] * y
                else:
                    t = d[f, i - 1] * y
                    q[...] += fold(t * y)
                f_o[f, i] = t

    fields(x0.shape[0], one)


def norm_body(v0, v1, v2, v3, q):
    q[...] = jnp.zeros_like(q)

    def one(f):
        for v, off in ((v0, 0), (v1, 1), (v2, 0), (v3, 1)):
            for i in range(3):
                x = v[f, i + off]
                q[...] += fold(x * x)

    fields(v0.shape[0], one)


def resid_body(sc, v0, v1, g0, g1, g2, g3, z2, z3, r2, r3, q):
    a = first_step(sc)
    q[...] = jnp.zeros_like(q)

    def dots(r, g):
        q[0] += fold(r * r)
        q[1] += fold(r * g)

    def one(f):
        for i in range(5):
            r = (1.0 - a) * g3[f, i] - a * z3[f, i]
            r3[f, i] = r
            if 0 < i < 4:
                dots(r, g3[f, i])
                dots(v1[f, i], g1[f, i])
        for i in range(3):
            r = (1.0 - a) * g2[f, i] - a * z2[f, i]
            r2[f, i] = r
            dots(r, g2[f, i])
            dots(v0[f, i], g0[f, i])

    fields(v0.shape[0], one)


def final_body(kind, c_ref, s1, s2, s3, *refs):
    r = refs[0:4]
    g = refs[4:8]
    n = 8
    if kind == "res":
        z = refs[8:12]
        n = 12
    keep, send = refs[n:]
    c = c_ref[0]
    rr0, rr1 = tot(s1, 0), tot(s2, 0)
    a0 = rr0 / (rr0 + tot(s1, 1))
    beta = rr1 / rr0
    a1 = rr1 / (rr1 + beta * (2.0 * tot(s2, 1) + beta * rr0) + tot(s3, 0))

    def one(f):
        for k in range(4):
            off = k % 2
            for i in range(3):
                res = r[k][f, i + off][PAD:-PAD]
                grad = g[k][f, i + off][PAD:-PAD]
                d = res + beta * grad
                if kind == "res":
                    val = res - a1 * (d + z[k][f, i + off][PAD:-PAD])
                else:
                    val = a0 * grad + a1 * d

                @pl.when(c == k // 2)
                def _():
                    keep[k % 2, f, i] = val

                @pl.when(c != k // 2)
                def _():
                    send[k % 2, f, i] = val

    fields(g[0].shape[0], one)


def join_body(half, n, c_ref, *refs):
    keep, other, out, sem = refs[:n], refs[n : 2 * n], refs[2 * n], refs[2 * n + 1]
    mine = pl.multiple_of(c_ref[0] * half, PAD)
    theirs = pl.multiple_of((1 - c_ref[0]) * half, PAD)
    copies = []
    for src, at in ((keep, mine), (other, theirs)):
        f0 = 0
        for s in src:
            nf = s.shape[1]
            for w in range(2):
                copies.append(
                    pltpu.make_async_copy(
                        s.at[w],
                        out.at[w, 0, pl.ds(f0, nf), :, pl.ds(at, half), :],
                        sem.at[len(copies)],
                    )
                )
            f0 += nf
    for cp in copies:
        cp.start()
    for cp in copies:
        cp.wait()


def per_device(winds, mixing, innovations, obs_weight, obs_sub, obs_col, obs_count):
    owners, slots = obs_sub.shape[2], obs_sub.shape[3]
    lev = mixing.shape[0]
    cols = winds.shape[4]
    half = cols // 2
    wide = half + 2 * PAD
    cells = winds.shape[3] * cols
    c = lax.axis_index("tm").astype(jnp.int32)
    pos = lax.axis_index("space")
    bands = lax.axis_size("space")
    c_arr = c.reshape(1)
    flags = jnp.stack([(pos > 0), (pos < bands - 1)]).astype(F32)
    north = [(i, (i + 1) % bands) for i in range(bands)]
    south = [((i + 1) % bands, i) for i in range(bands)]

    def swap(x):
        return lax.ppermute(x, "tm", [(0, 1), (1, 0)])

    def exchange(ss, sn):
        return lax.ppermute(sn, "space", north), lax.ppermute(ss, "space", south)

    def total(parts):
        vals = swap(parts) + parts
        step = 1
        while step < bands:
            vals = vals + lax.ppermute(
                vals, "space", [(i, i ^ step) for i in range(bands)]
            )
            step *= 2
        return vals

    live = (
        jnp.arange(slots, dtype=jnp.int32)[None, :] < obs_count.reshape(owners)[:, None]
    )
    place = (obs_sub * cells + obs_col).reshape(owners, slots)
    place = jnp.where(live, place, -1).astype(F32)
    place = jnp.broadcast_to(place[..., None], (owners, slots, lev))
    blocks = 2 * FIELDS + 1
    packed = call(
        pack_body,
        (
            obs_weight.reshape(owners, slots, -1),
            innovations.reshape(owners, slots, -1),
            place,
        ),
        [VM] * 3,
        [sds(owners, blocks, slots, lev)],
    )[0]
    got = lax.all_to_all(packed, "space", split_axis=0, concat_axis=0, tiled=True)

    w_own, w_snd, ra, rf = call(
        functools.partial(wind_body, half),
        (c_arr, winds[:, 0], mixing),
        [SM, VM, VM],
        [sds(2, 2, 3, wide, lev)] * 2 + [sds(2 * lev, 2 * lev, dtype=BF16)] * 2,
    )
    w_got = swap(w_snd)
    w0, w1, w2, w3, down, up = call(
        pick_wind_body,
        (c_arr, w_own, w_got),
        [SM, VM, VM],
        [sds(2, 3, wide, lev)] * 4 + [sds(2, wide, lev)] * 2,
    )
    from_s, from_n = exchange(down, up)
    from_s = jnp.where(pos > 0, from_s, 0.0)
    from_n = jnp.where(pos < bands - 1, from_n, 0.0)
    wh0 = jnp.stack([from_s[0], from_n[0]])
    wh2 = jnp.stack([from_s[1], from_n[1]])

    idx = jnp.maximum(got[:, 2 * FIELDS, :, 0], 0.0).astype(jnp.int32)
    d_own, d_snd, g_own, g_snd = call(
        functools.partial(scatter_body, half),
        (c_arr, idx, got.reshape(owners * blocks * slots, lev)),
        [SM, SM, VM],
        [sds(2, FIELDS, 3, wide, lev)] * 4,
        scratch=[pltpu.VMEM((2 * cells * 8, lev), F32)],
        vmem=16 * 2**20,
    )
    g_got = swap(g_snd)
    d_got = swap(d_snd)
    groups = []
    f0 = 0
    for nf in GROUPS:
        shapes = [sds(nf, 3, wide, lev)] * 4
        pick = functools.partial(pick_body, f0)
        gg = call(pick, (c_arr, g_own, g_got), [SM, VM, VM], shapes)
        dd = call(pick, (c_arr, d_own, d_got), [SM, VM, VM], shapes)
        ds, dn = exchange(
            jnp.stack([dd[0][:, 0], dd[2][:, 0]]), jnp.stack([dd[0][:, 2], dd[2][:, 2]])
        )
        groups.append((nf, gg, dd, ds, dn))
        f0 += nf

    part = sds(8, lev)

    def row3(nf):
        return sds(nf, 3, wide, lev)

    def row5(nf):
        return sds(nf, 5, wide, lev)

    def state_of(nf, n):
        return [sds(nf, wide, lev)] + [sds(n, nf, wide, lev)] * 2

    def adj_mid(state, f2, f1, g0=None):
        mid, ss, sn = state
        nf = mid.shape[0]
        rs, rn = exchange(ss, sn)
        ext = g0 is not None
        n = 3 if ext else 2
        ins = (flags, mid, ss, sn, rs, rn, f2, f1, w2, wh2, w1, ra) + ((g0,) if ext else ())
        o = call(
            functools.partial(adj_mid_body, ext),
            ins,
            [SM] + [VM] * (len(ins) - 1),
            [row5(nf), row3(nf)] + state_of(nf, n),
        )
        return o[0], o[1], tuple(o[2:])

    def adj_last(mode, state, f0, extra=()):
        mid, ss, sn = state
        nf = mid.shape[0]
        rs, rn = exchange(ss, sn)
        ins = (flags, mid, ss, sn, rs, rn, f0, w0, wh0, ra) + extra
        specs = [SM] + [VM] * 9 + ([VM] * 3 if extra else [])
        outs = [row3(nf), row5(nf)] + (state_of(nf, 2) if mode < 2 else [])
        o = call(functools.partial(adj_last_body, mode), ins, specs, outs)
        return o[0], o[1], tuple(o[2:])

    def fwd_first(state, v1, v2):
        mid, ss, sn = state
        nf = mid.shape[0]
        rs, rn = exchange(ss, sn)
        ins = (flags, mid, ss, sn, rs, rn, v1, v2, w0, wh0, w1, w2, rf)
        o = call(
            fwd_first_body,
            ins,
            [SM] + [VM] * 12,
            [row5(nf), row3(nf)] + state_of(nf, 2),
        )
        return o[0], o[1], tuple(o[2:])

    def fwd_last(state, v3, x0, x1):
        mid, ss, sn = state
        nf = mid.shape[0]
        rs, rn = exchange(ss, sn)
        ins = (flags, mid, ss, sn, rs, rn, v3, x0, x1, w2, wh2, w3, rf)
        return call(
            functools.partial(fwd_last_body, half),
            ins,
            [SM] + [VM] * 12,
            [row5(nf), row3(nf), sds(nf, 16, 2 * PAD, lev)],
        )

    def turn(xs, eg, dd, ds, dn, sums=(), old=None):
        eg = swap(eg)
        second = old is not None
        x0, x1, x2, x3 = xs
        nf = x3.shape[0]
        ex = sums + (old[3],) if second else ()
        o = call(
            functools.partial(turn_body, second),
            (x3, eg, dd[3], w3, ra) + ex,
            [VM] * (5 + len(ex)),
            [row3(nf)] + state_of(nf, 2) + [part],
        )
        y3, state, q3 = o[0], tuple(o[1:4]), o[4]
        ex = sums + tuple(old[:3]) if second else ()
        y0, y1, y2, f0, f1, f2, q = call(
            functools.partial(rest_body, second),
            (x0, x1, x2, eg, dd[0], dd[1], dd[2], ds, dn) + ex,
            [VM] * (9 + len(ex)),
            [row5(nf), row3(nf), row5(nf)] * 2 + [part],
        )
        return state, (y0, y1, y2, y3), (f0, f1, f2), q3 + q

    def forward(state, v):
        x0, x1, state = fwd_first(state, v[1], v[2])
        x2, x3, eg = fwd_last(state, v[3], x0, x1)
        return (x0, x1, x2, x3), eg

    grads, mids = [], []
    for nf, gg, dd, ds, dn in groups:
        state = tuple(
            call(turn_first_body, (gg[3], gg[2], w3, ra), [VM] * 4, state_of(nf, 3))
        )
        g3, g2, state = adj_mid(state, gg[2], gg[1], gg[0])
        g0, g1, state = adj_last(0, state, gg[0])
        g = (g0, g1, g2, g3)
        rr = call(norm_body, g, [VM] * 4, [part])[0]
        xs, eg = forward(state, g)
        state, ys, fs, q = turn(xs, eg, dd, ds, dn)
        grads.append(g)
        mids.append((state, ys, fs, rr, q))
    s1 = total(jnp.stack([sum(m[3] for m in mids), sum(m[4] for m in mids)]))

    resid, ends = [], []
    for g, (state, _, fs, _, _) in zip(grads, mids):
        nf = g[0].shape[0]
        z3, z2, state = adj_mid(state, fs[2], fs[1])
        v0, v1, state = adj_last(1, state, fs[0], (s1, g[0], g[1]))
        v2, v3, q = call(
            resid_body,
            (s1, v0, v1) + g + (z2, z3),
            [VM] * 9,
            [row3(nf), row5(nf), sds(2, 8, lev)],
        )
        v = (v0, v1, v2, v3)
        resid.append(v)
        ends.append((forward(state, v), q))
    s2 = total(sum(e[1] for e in ends))

    turns = []
    for ((xs, eg), _), (_, ys, _, _, _), (nf, gg, dd, ds, dn) in zip(ends, mids, groups):
        turns.append(turn(xs, eg, dd, ds, dn, (s1, s2), ys))
    s3 = total(sum(t[3] for t in turns)[None])

    def final(kind, v, g, z=()):
        nf = g[0].shape[0]
        ins = (c_arr, s1, s2, s3) + tuple(v) + tuple(g) + tuple(z)
        shape = sds(2, nf, 3, half, lev)
        keep, send = call(
            functools.partial(final_body, kind),
            ins,
            [SM] + [VM] * (len(ins) - 1),
            [shape, shape],
        )
        return keep, swap(send)

    def join(parts):
        n = len(parts)
        ins = (c_arr,) + tuple(p[0] for p in parts) + tuple(p[1] for p in parts)
        return call(
            functools.partial(join_body, half, n),
            ins,
            [SM] + [VM] * (2 * n),
            [sds(2, 1, FIELDS, 3, cols, lev)],
            scratch=[pltpu.SemaphoreType.DMA((4 * n,))],
            out_specs=[pl.BlockSpec(memory_space=pl.ANY)],
        )[0]

    increment = join([final("inc", v, g) for v, g in zip(resid, grads)])
    parts = []
    for v, g, (state, _, fs, _) in zip(resid, grads, turns):
        z3, z2, state = adj_mid(state, fs[2], fs[1])
        z0, z1, _ = adj_last(2, state, fs[0])
        parts.append(final("res", v, g, (z0, z1, z2, z3)))
    return increment, join(parts)


def solution(mesh):
    in_specs = (
        P("tm", "space", None, None, None, None),
        P(),
        P("tm", "space", None, None, None),
        P("tm", "space", None, None, None),
        P("tm", "space", None, None),
        P("tm", "space", None, None),
        P("tm", "space", None),
    )
    out_specs = (P("tm", "space", None, None, None, None), P("tm", "space", None, None, None, None))
    return jax.shard_map(
        per_device, mesh=mesh, in_specs=in_specs, out_specs=out_specs, check_vma=False
    )
```

```python
import functools
import jax
import jax.numpy as jnp
from jax import lax
from jax.experimental import pallas as pl
from jax.experimental.pallas import tpu as pltpu
from jax.sharding import PartitionSpec as P

FIELDS = 3
MIXC = 0.25
SCALE_Q = 0.5
GROUPS = (3,)
PAD = 8
F32 = jnp.float32
BF16 = jnp.bfloat16

VM = pl.BlockSpec(memory_space=pltpu.VMEM)
SM = pl.BlockSpec(memory_space=pltpu.SMEM)


def call(body, ins, specs, outs, vmem=None, flops=1e8, scratch=(), out_specs=None):
    nbytes = sum(a.size * a.dtype.itemsize for a in ins)
    nbytes += sum(o.size * o.dtype.itemsize for o in outs)
    return pl.pallas_call(
        body,
        out_shape=outs,
        in_specs=specs,
        out_specs=out_specs or [VM] * len(outs),
        scratch_shapes=list(scratch),
        compiler_params=pltpu.CompilerParams(vmem_limit_bytes=vmem or 6 * 2**20),
        cost_estimate=pl.CostEstimate(
            flops=int(flops), bytes_accessed=int(nbytes), transcendentals=0
        ),
    )(*ins)


def sds(*shape, dtype=F32):
    return jax.ShapeDtypeStruct(shape, dtype)


def later(x):
    return pltpu.roll(x, 1, 0)


def earlier(x):
    return pltpu.roll(x, x.shape[0] - 1, 0)


def coef(w_ref, i):
    a = w_ref[0, i]
    b = w_ref[1, i]
    ap = jnp.maximum(a, 0.0)
    am = ap - a
    bp = jnp.maximum(b, 0.0)
    bm = bp - b
    return ap, am, bp, bm, 1.0 - (ap + am) - (bp + bm)


def mixed(v, rhs):
    lev = v.shape[1]
    hi = v.astype(BF16)
    lo = (v - hi.astype(F32)).astype(BF16)
    o = jnp.dot(jnp.concatenate([hi, lo], axis=1), rhs, preferred_element_type=F32)
    return v + (o[:, :lev] + o[:, lev:])


def adj_local(w, c):
    ap, am, _, _, c0 = c
    return c0 * w + earlier(ap * w) + later(am * w)


def fwd_local(u, c):
    ap, am, _, _, c0 = c
    return c0 * u + ap * later(u) + am * earlier(u)


def adj_pre(f, rows, w_ref, rhs, mid_ref, ss_ref, sn_ref):
    w = [mixed(x, rhs) for x in rows]
    c = [coef(w_ref, i) for i in range(3)]
    mid_ref[f] = adj_local(w[1], c[1]) + c[2][2] * w[2] + c[0][3] * w[0]
    ss_ref[0, f] = adj_local(w[0], c[0]) + c[1][2] * w[1]
    ss_ref[1, f] = c[0][2] * w[0]
    sn_ref[0, f] = adj_local(w[2], c[2]) + c[1][3] * w[1]
    sn_ref[1, f] = c[2][3] * w[2]


def adj_post(f, mid_ref, ss_ref, sn_ref, rs_ref, rn_ref, fs, fn):
    return [
        (rs_ref[0, f] + ss_ref[1, f]) * fs,
        ss_ref[0, f] + rs_ref[1, f] * fs,
        mid_ref[f],
        sn_ref[0, f] + rn_ref[1, f] * fn,
        (rn_ref[0, f] + sn_ref[1, f]) * fn,
    ]


def adj_second(rows5, w_ref, wh_ref, rhs):
    w = [mixed(x, rhs) for x in rows5]
    c = [coef(w_ref, i) for i in range(3)]
    up = [c[1][2], c[2][2], wh_ref[1]]
    down = [wh_ref[0], c[0][3], c[1][3]]
    return [
        adj_local(w[i + 1], c[i]) + up[i] * w[i + 2] + down[i] * w[i] for i in range(3)
    ]


def fwd_pre(f, u, w_ref, mid_ref, ss_ref, sn_ref):
    c = [coef(w_ref, i) for i in range(3)]
    mid_ref[f] = fwd_local(u[1], c[1]) + c[1][2] * u[0] + c[1][3] * u[2]
    ss_ref[0, f] = u[0]
    ss_ref[1, f] = fwd_local(u[0], c[0]) + c[0][3] * u[1]
    sn_ref[0, f] = u[2]
    sn_ref[1, f] = fwd_local(u[2], c[2]) + c[2][2] * u[1]


def fwd_post(f, mid_ref, ss_ref, sn_ref, rs_ref, rn_ref, w_ref, wh_ref, fs, fn, rhs):
    b0 = w_ref[1, 0]
    b2 = w_ref[1, 2]
    m = [
        rs_ref[1, f] * fs + wh_ref[0] * ss_ref[0, f],
        ss_ref[1, f] + jnp.maximum(b0, 0.0) * (rs_ref[0, f] * fs),
        mid_ref[f],
        sn_ref[1, f] + jnp.maximum(-b2, 0.0) * (rn_ref[0, f] * fn),
        rn_ref[1, f] * fn + wh_ref[1] * sn_ref[0, f],
    ]
    return [mixed(x, rhs) for x in m]


def fwd_second(u5, w_ref, rhs):
    out = []
    for i in range(3):
        c = coef(w_ref, i)
        m = fwd_local(u5[i + 1], c) + c[2] * u5[i] + c[3] * u5[i + 2]
        out.append(mixed(m, rhs))
    return out


def fields(n, body):
    if n == 1:
        body(0)
        return

    def step(f, carry):
        body(f)
        return carry

    lax.fori_loop(0, n, step, 0)


def fold(x):
    own = x[PAD:-PAD]
    return jnp.sum(own.reshape(own.shape[0] // 8, 8, own.shape[1]), axis=0)


def split_store(x, half, c, own_ref, snd_ref, idx):
    n = x.shape[0]
    low = jnp.concatenate([x[n - PAD :], x[: half + PAD]], axis=0)
    high = jnp.concatenate([x[half - PAD :], x[:PAD]], axis=0)

    @pl.when(c == 0)
    def _():
        own_ref[idx] = low
        snd_ref[idx] = high

    @pl.when(c != 0)
    def _():
        own_ref[idx] = high
        snd_ref[idx] = low


def pack_body(w_ref, d_ref, i_ref, o_ref):
    lev = o_ref.shape[-1]
    live = i_ref[...] >= 0.0
    for f in range(FIELDS):
        w = jnp.where(live, w_ref[:, :, f * lev : (f + 1) * lev], 0.0)
        o_ref[:, f] = w
        o_ref[:, FIELDS + f] = w * d_ref[:, :, f * lev : (f + 1) * lev]
    o_ref[:, 2 * FIELDS] = i_ref[...]


def emit(half, c, acc, at, own_ref, snd_ref):
    cols = 2 * half
    for w in range(2):

        def one(i, carry):
            base = (w * 3 + i) * (cols * 8) + at
            for f in range(FIELDS):
                x = acc[pl.ds(base + f, cols, stride=8), :]
                split_store(x, half, c, own_ref, snd_ref, (w, f, i))
            return carry

        lax.fori_loop(0, 3, one, 0)


def scatter_body(half, c_ref, idx_ref, p_ref, acc, go_ref, gs_ref):
    owners, slots = idx_ref.shape
    blocks = 2 * FIELDS + 1
    lev = p_ref.shape[1]
    cells = acc.shape[0] // 8
    chunk = 64

    def clear(t, carry):
        acc[pl.ds(pl.multiple_of(t * (8 * chunk), 8 * chunk), 8 * chunk), :] = jnp.zeros(
            (8 * chunk, lev), F32
        )
        return carry

    lax.fori_loop(0, cells // chunk, clear, 0)

    def put(o, carry):
        for s in range(slots):
            row = pl.multiple_of(idx_ref[o, s] * 8, 8)
            x = p_ref[pl.ds(o * (blocks * slots) + s, blocks, stride=slots), :]
            acc[pl.ds(row, blocks), :] += x
        return carry

    lax.fori_loop(0, owners, put, 0)
    emit(half, c_ref[0], acc, FIELDS, go_ref, gs_ref)


def diag_body(half, c_ref, acc, do_ref, ds_ref):
    emit(half, c_ref[0], acc, 0, do_ref, ds_ref)


def wind_body(half, c_ref, w_ref, m_ref, o_ref, s_ref, ra_ref, rf_ref):
    c = c_ref[0]
    for w in range(2):

        def one(i, carry):
            for k in range(2):
                split_store(w_ref[w, k, i].astype(F32), half, c, o_ref, s_ref, (w, k, i))
            return carry

        lax.fori_loop(0, 3, one, 0)
    for m, ref in ((m_ref[...] * MIXC, ra_ref), (m_ref[...].T * MIXC, rf_ref)):
        hi = m.astype(BF16)
        lo = (m - hi.astype(F32)).astype(BF16)
        line = jnp.concatenate([hi, lo], axis=1)
        ref[...] = jnp.concatenate([line, line], axis=0)


def pick_body(f0, c_ref, own_ref, got_ref, *outs):
    c = c_ref[0]
    nf = outs[0].shape[0]

    def put(src, dst):
        for w in range(2):
            for f in range(nf):
                dst[w][f] = src[w, f0 + f]

    @pl.when(c == 0)
    def _():
        put(own_ref, outs[:2])
        put(got_ref, outs[2:4])

    @pl.when(c != 0)
    def _():
        put(got_ref, outs[:2])
        put(own_ref, outs[2:4])


def pick_wind_body(c_ref, own_ref, got_ref, w0, w1, w2, w3, ss, sn):
    pick_body(0, c_ref, own_ref, got_ref, w0, w1, w2, w3)
    for k, w in enumerate((w0, w2)):
        ss[k] = jnp.maximum(w[1, 0], 0.0)
        sn[k] = jnp.maximum(-w[1, 2], 0.0)


def turn_first_body(g3_ref, g2_ref, w3_ref, ra_ref, mid_ref, ss_ref, sn_ref):
    rhs = ra_ref[...]

    def one(f):
        adj_pre(f, [g3_ref[f, i] for i in range(3)], w3_ref, rhs, mid_ref, ss_ref, sn_ref)
        ss_ref[2, f] = g2_ref[f, 0]
        sn_ref[2, f] = g2_ref[f, 2]

    fields(g3_ref.shape[0], one)


def five(f, f_ref, rs_ref, rn_ref, ext):
    if ext:
        return [rs_ref[2, f]] + [f_ref[f, i] for i in range(3)] + [rn_ref[2, f]]
    return [f_ref[f, i] for i in range(5)]


def adj_mid_body(ext, carry, *refs):
    if carry:
        refs[-1][...] = refs[12][...]
        refs = refs[:12] + refs[13:-1]
    (fl, mid, ss, sn, rs, rn, f2, f1, w2, wh2, w1, ra) = refs[:12]
    n = 12
    if ext:
        g0 = refs[n]
        n += 1
    g3, g2, mid_o, ss_o, sn_o = refs[n:]
    fs, fn = fl[0], fl[1]
    rhs = ra[...]

    def one(f):
        lam = adj_post(f, mid, ss, sn, rs, rn, fs, fn)
        for i in range(5):
            g3[f, i] = lam[i] * SCALE_Q
        src = five(f, f2, rs, rn, ext)
        out = adj_second([lam[i] + src[i] for i in range(5)], w2, wh2, rhs)
        for i in range(3):
            g2[f, i] = out[i] * SCALE_Q
        adj_pre(f, [out[i] + f1[f, i] for i in range(3)], w1, rhs, mid_o, ss_o, sn_o)
        if ext:
            ss_o[2, f] = g0[f, 0]
            sn_o[2, f] = g0[f, 2]

    fields(mid.shape[0], one)


def adj_last_body(mode, *refs):
    (fl, mid, ss, sn, rs, rn, f0, w0, wh0, ra) = refs[:10]
    outs = refs[10:]
    fs, fn = fl[0], fl[1]
    rhs = ra[...]

    def one(f):
        lam = adj_post(f, mid, ss, sn, rs, rn, fs, fn)
        src = five(f, f0, rs, rn, mode == 0)
        out = adj_second([lam[i] + src[i] for i in range(5)], w0, wh0, rhs)
        for i in range(5):
            outs[1][f, i] = lam[i] * SCALE_Q
        for i in range(3):
            outs[0][f, i] = out[i]
        if mode < 2:
            fwd_pre(f, out, w0, *outs[2:5])

    fields(mid.shape[0], one)


def fwd_first_body(fl, mid, ss, sn, rs, rn, v1, v2, w0, wh0, w1, w2, rf, *outs):
    x0, x1, mid_o, ss_o, sn_o = outs
    fs, fn = fl[0], fl[1]
    rhs = rf[...]

    def one(f):
        x5 = fwd_post(f, mid, ss, sn, rs, rn, w0, wh0, fs, fn, rhs)
        for i in range(5):
            x0[f, i] = x5[i]
        x3 = fwd_second([x5[i] + SCALE_Q * v1[f, i] for i in range(5)], w1, rhs)
        for i in range(3):
            x1[f, i] = x3[i]
        fwd_pre(f, [x3[i] + SCALE_Q * v2[f, i] for i in range(3)], w2, mid_o, ss_o, sn_o)

    fields(mid.shape[0], one)


def edge(x, half):
    return jnp.concatenate([x[half : half + PAD], x[PAD : 2 * PAD]], axis=0)


def fwd_last_body(half, fl, mid, ss, sn, rs, rn, v3, x0, x1, w2, wh2, w3, rf, *outs):
    x2, x3, eg = outs
    fs, fn = fl[0], fl[1]
    rhs = rf[...]

    def one(f):
        x5 = fwd_post(f, mid, ss, sn, rs, rn, w2, wh2, fs, fn, rhs)
        for i in range(5):
            x2[f, i] = x5[i]
            eg[f, 8 + i] = edge(x5[i], half)
            eg[f, i] = edge(x0[f, i], half)
        y3 = fwd_second([x5[i] + SCALE_Q * v3[f, i] for i in range(5)], w3, rhs)
        for i in range(3):
            x3[f, i] = y3[i]
            eg[f, 13 + i] = edge(y3[i], half)
            eg[f, 5 + i] = edge(x1[f, i], half)

    fields(mid.shape[0], one)


def fixed(x, e):
    return jnp.concatenate([e[:PAD], x[PAD:-PAD], e[PAD:]], axis=0)


def turn_body(carry, sc, x3, eg, d3, w3, ra, *outs):
    if carry:
        outs[4][...] = outs[0][...]
        outs = outs[1:4]
    mid, ss, sn = outs[:3]
    q = None if carry else outs[3]
    rhs = ra[...]
    if q is not None:
        q[...] = jnp.zeros_like(q)
    scale = sc[0]

    def one(f):
        rows = []
        for i in range(3):
            y = fixed(x3[f, i], eg[f, 13 + i])
            t = d3[f, i] * y
            if q is not None:
                q[...] += fold(t * y)
            rows.append(t * scale)
        adj_pre(f, rows, w3, rhs, mid, ss, sn)

    fields(x3.shape[0], one)


def rest_body(sc, x0, x1, x2, eg, d0, d1, d2, ds, dn, f0, f1, f2, q=None):
    if q is not None:
        q[...] = jnp.zeros_like(q)
    scale = sc[0]

    def one(f):
        for x, rows, at, d, w, f_o in (
            (x0, 5, 0, d0, 0, f0),
            (x1, 3, 5, d1, None, f1),
            (x2, 5, 8, d2, 1, f2),
        ):
            for i in range(rows):
                y = fixed(x[f, i], eg[f, at + i])
                if rows == 5 and i == 0:
                    t = ds[w, f] * y
                elif rows == 5 and i == 4:
                    t = dn[w, f] * y
                else:
                    t = d[f, i - (rows == 5)] * y
                    if q is not None:
                        q[...] += fold(t * y)
                f_o[f, i] = t * scale

    fields(x0.shape[0], one)


def norm_body(v0, v1, v2, v3, q):
    q[...] = jnp.zeros_like(q)

    def one(f):
        for v, off in ((v0, 0), (v1, 1), (v2, 0), (v3, 1)):
            for i in range(3):
                x = v[f, i + off]
                q[...] += fold(x * x)

    fields(v0.shape[0], one)


def lanes(shape):
    return lax.broadcasted_iota(jnp.int32, shape, len(shape) - 1)


def sums_body(n, *refs):
    out = refs[-1]
    parts = [refs[:n], refs[n : 3 * n], refs[3 * n : 4 * n]]
    acc = jnp.zeros(refs[0].shape, F32)
    at = 4 * n
    for _ in range(n):
        xs, ds = refs[at : at + 4], refs[at + 4 : at + 8]
        at += 8

        def one(f, acc):
            for x, d in zip(xs, ds):
                off = (x.shape[1] - 3) // 2
                for i in range(3):
                    v = x[f, i + off]
                    acc = acc + fold(d[f, i] * v * v)
            return acc

        nf = xs[0].shape[0]
        acc = one(0, acc) if nf == 1 else lax.fori_loop(0, nf, one, acc)
    lane = lanes(out.shape)
    row = jnp.where(lane == 3, jnp.sum(acc, keepdims=True), 0.0)
    for k in range(3):
        val = parts[k][0][...]
        for p in parts[k][1:]:
            val = val + p[...]
        row = jnp.where(lane == k, jnp.sum(val, keepdims=True), row)
    out[...] = row


def add_body(a, b, out):
    out[...] = a[...] + b[...]


def ring_body(step, pos_ref, a, b, c, d, out):
    mine = lax.rem(lax.div(pos_ref[0], step), 4)
    rows = [a[...], b[...], c[...], d[...]]
    total = jnp.zeros(out.shape, F32)
    for place in range(4):
        gap = lax.rem(mine + 4 - place, 4)
        term = rows[0]
        for k in (1, 2, 3):
            term = jnp.where(gap == k, rows[k], term)
        total = total + term
    out[...] = total


def solve_body(hs, got, out):
    row = got[...]
    at = lanes(row.shape)

    def pick(k):
        return jnp.sum(jnp.where(at == k, row, 0.0), axis=1, keepdims=True)

    rr, bg, zz, bz = [pick(k) for k in range(4)]
    sig, inv = hs[0], hs[1]
    a0 = rr / (rr + bg)
    left = bg / (rr + bg)
    c = a0 * inv
    sbg = bg * sig
    rr1 = c * (c * (zz - sbg * (sbg / rr)))
    beta = rr1 / rr
    p = left + beta
    curve = p * (p * bg) - 2.0 * (p * (c * (inv * zz))) + c * (c * bz)
    a1 = rr1 / (rr1 + beta * beta * rr + curve)
    terms = (
        a0 + a1 * p,
        -(a1 * c),
        left - a1 * p,
        a1 * c - c - a1 * (p * inv),
        a1 * c,
    )
    w = jnp.zeros(row.shape, F32)
    for k, t in enumerate(terms):
        w = jnp.where(at == k, t, w)
    out[...] = w


def final_body(kind, c_ref, k_ref, *refs):
    row = k_ref[...]
    at = lanes(row.shape)

    def pick(k):
        return jnp.sum(jnp.where(at == k, row, 0.0), axis=1, keepdims=True)

    g, z = refs[0:4], refs[4:8]
    n = 8
    if kind == "res":
        w = refs[8:12]
        n = 12
        kg, kz, kw = pick(2), pick(3), pick(4)
    else:
        kg, kz = pick(0), pick(1)
    keep, send = refs[n:]
    c = c_ref[0]

    def one(f):
        for k in range(4):
            off = k % 2
            for i in range(3):
                val = kg * g[k][f, i + off][PAD:-PAD] + kz * z[k][f, i + off][PAD:-PAD]
                if kind == "res":
                    val = val + kw * w[k][f, i + off][PAD:-PAD]

                @pl.when(c == k // 2)
                def _():
                    keep[k % 2, f, i] = val

                @pl.when(c != k // 2)
                def _():
                    send[k % 2, f, i] = val

    fields(g[0].shape[0], one)


def join_body(half, n, c_ref, *refs):
    keep, other, out, sem = refs[:n], refs[n : 2 * n], refs[2 * n], refs[2 * n + 1]
    mine = pl.multiple_of(c_ref[0] * half, PAD)
    theirs = pl.multiple_of((1 - c_ref[0]) * half, PAD)
    copies = []
    for src, at in ((keep, mine), (other, theirs)):
        f0 = 0
        for s in src:
            nf = s.shape[1]
            for w in range(2):
                copies.append(
                    pltpu.make_async_copy(
                        s.at[w],
                        out.at[w, 0, pl.ds(f0, nf), :, pl.ds(at, half), :],
                        sem.at[len(copies)],
                    )
                )
            f0 += nf
    for cp in copies:
        cp.start()
    for cp in copies:
        cp.wait()


def per_device(winds, mixing, innovations, obs_weight, obs_sub, obs_col, obs_count):
    owners, slots = obs_sub.shape[2], obs_sub.shape[3]
    lev = mixing.shape[0]
    cols = winds.shape[4]
    half = cols // 2
    wide = half + 2 * PAD
    cells = winds.shape[3] * cols
    c = lax.axis_index("tm").astype(jnp.int32)
    pos = lax.axis_index("space")
    bands = lax.axis_size("space")
    c_arr = c.reshape(1)
    pos_arr = pos.astype(jnp.int32).reshape(1)
    flags = jnp.stack([(pos > 0), (pos < bands - 1)]).astype(F32)
    north = [(i, (i + 1) % bands) for i in range(bands)]
    south = [((i + 1) % bands, i) for i in range(bands)]

    def swap(x):
        return lax.ppermute(x, "tm", [(0, 1), (1, 0)])

    def exchange(ss, sn):
        return lax.ppermute(sn, "space", north), lax.ppermute(ss, "space", south)

    def ring_sum(row, step):
        shifts = []
        for k in (1, 2, 3):
            pairs = []
            for i in range(bands):
                digit = (i // step) % 4
                pairs.append((i, i + ((digit + k) % 4 - digit) * step))
            shifts.append(pairs)
        got = tuple(lax.ppermute(row, "space", p) for p in shifts)
        return call(
            functools.partial(ring_body, step),
            (pos_arr, row) + got,
            [SM] + [VM] * 4,
            [sds(1, lev)],
            flops=1e5,
        )[0]

    live = (
        jnp.arange(slots, dtype=jnp.int32)[None, :] < obs_count.reshape(owners)[:, None]
    )
    place = (obs_sub * cells + obs_col).reshape(owners, slots)
    place = jnp.where(live, place, -1).astype(F32)
    place = jnp.broadcast_to(place[..., None], (owners, slots, lev))
    blocks = 2 * FIELDS + 1
    packed = call(
        pack_body,
        (
            obs_weight.reshape(owners, slots, -1),
            innovations.reshape(owners, slots, -1),
            place,
        ),
        [VM] * 3,
        [sds(owners, blocks, slots, lev)],
    )[0]
    got = lax.all_to_all(packed, "space", split_axis=0, concat_axis=0, tiled=True)

    w_own, w_snd, ra, rf = call(
        functools.partial(wind_body, half),
        (c_arr, winds[:, 0], mixing),
        [SM, VM, VM],
        [sds(2, 2, 3, wide, lev)] * 2 + [sds(2 * lev, 2 * lev, dtype=BF16)] * 2,
    )
    w_got = swap(w_snd)
    w0, w1, w2, w3, down, up = call(
        pick_wind_body,
        (c_arr, w_own, w_got),
        [SM, VM, VM],
        [sds(2, 3, wide, lev)] * 4 + [sds(2, wide, lev)] * 2,
    )
    from_s, from_n = exchange(down, up)
    from_s = jnp.where(pos > 0, from_s, 0.0)
    from_n = jnp.where(pos < bands - 1, from_n, 0.0)
    wh0 = jnp.stack([from_s[0], from_n[0]])
    wh2 = jnp.stack([from_s[1], from_n[1]])

    size = jnp.abs(mixing)
    grow = (1.0 + MIXC * jnp.max(jnp.sum(size, 0))) * (1.0 + MIXC * jnp.max(jnp.sum(size, 1)))
    grow = grow * grow
    inv = grow * grow
    sig = 1.0 / inv
    sig_arr = sig.reshape(1)
    one_arr = jnp.ones((1,), F32)
    span = jnp.stack([sig, 1.0 / sig])

    idx = jnp.maximum(got[:, 2 * FIELDS, :, 0], 0.0).astype(jnp.int32)
    idx, wh0, wh2, w0, w1, w2, w3, sig_arr, span = lax.optimization_barrier(
        (idx, wh0, wh2, w0, w1, w2, w3, sig_arr, span)
    )
    halves = [sds(2, FIELDS, 3, wide, lev)] * 2
    acc, g_own, g_snd = call(
        functools.partial(scatter_body, half),
        (c_arr, idx, got.reshape(owners * blocks * slots, lev)),
        [SM, SM, VM],
        [sds(2 * cells * 8, lev)] + halves,
    )
    g_got = swap(g_snd)
    d_own, d_snd = call(functools.partial(diag_body, half), (c_arr, acc), [SM, VM], halves)
    d_got = swap(d_snd)
    groups = []
    f0 = 0
    for nf in GROUPS:
        shapes = [sds(nf, 3, wide, lev)] * 4
        pick = functools.partial(pick_body, f0)
        gg = call(pick, (c_arr, g_own, g_got), [SM, VM, VM], shapes)
        dd = call(pick, (c_arr, d_own, d_got), [SM, VM, VM], shapes)
        ds, dn = exchange(
            jnp.stack([dd[0][:, 0], dd[2][:, 0]]), jnp.stack([dd[0][:, 2], dd[2][:, 2]])
        )
        groups.append((nf, gg, dd, ds, dn))
        f0 += nf

    part = sds(8, lev)

    def row3(nf):
        return sds(nf, 3, wide, lev)

    def row5(nf):
        return sds(nf, 5, wide, lev)

    def state_of(nf, n):
        return [sds(nf, wide, lev)] + [sds(n, nf, wide, lev)] * 2

    def adj_mid(state, f2, f1, g0=None, row=None):
        mid, ss, sn = state
        nf = mid.shape[0]
        rs, rn = exchange(ss, sn)
        ext = g0 is not None
        carry = row is not None
        n = 3 if ext else 2
        ins = (flags, mid, ss, sn, rs, rn, f2, f1, w2, wh2, w1, ra) + ((g0,) if ext else ())
        ins += (row,) if carry else ()
        o = call(
            functools.partial(adj_mid_body, ext, carry),
            ins,
            [SM] + [VM] * (len(ins) - 1),
            [row5(nf), row3(nf)] + state_of(nf, n) + ([sds(1, lev)] if carry else []),
        )
        if carry:
            return o[0], o[1], tuple(o[2:5]), o[5]
        return o[0], o[1], tuple(o[2:])

    def adj_last(mode, state, f0):
        mid, ss, sn = state
        nf = mid.shape[0]
        rs, rn = exchange(ss, sn)
        ins = (flags, mid, ss, sn, rs, rn, f0, w0, wh0, ra)
        specs = [SM] + [VM] * 9
        outs = [row3(nf), row5(nf)] + (state_of(nf, 2) if mode < 2 else [])
        o = call(functools.partial(adj_last_body, mode), ins, specs, outs)
        return o[0], o[1], tuple(o[2:])

    def fwd_first(state, v1, v2):
        mid, ss, sn = state
        nf = mid.shape[0]
        rs, rn = exchange(ss, sn)
        ins = (flags, mid, ss, sn, rs, rn, v1, v2, w0, wh0, w1, w2, rf)
        o = call(
            fwd_first_body,
            ins,
            [SM] + [VM] * 12,
            [row5(nf), row3(nf)] + state_of(nf, 2),
        )
        return o[0], o[1], tuple(o[2:])

    def fwd_last(state, v3, x0, x1):
        mid, ss, sn = state
        nf = mid.shape[0]
        rs, rn = exchange(ss, sn)
        ins = (flags, mid, ss, sn, rs, rn, v3, x0, x1, w2, wh2, w3, rf)
        return call(
            functools.partial(fwd_last_body, half),
            ins,
            [SM] + [VM] * 12,
            [row5(nf), row3(nf), sds(nf, 16, 2 * PAD, lev)],
        )

    def turn(xs, eg, dd, ds, dn, scale, row=None):
        eg = swap(eg)
        x0, x1, x2, x3 = xs
        nf = x3.shape[0]
        carry = row is not None
        o = call(
            functools.partial(turn_body, carry),
            (scale, x3, eg, dd[3], w3, ra) + ((row,) if carry else ()),
            [SM] + [VM] * (6 if carry else 5),
            state_of(nf, 2) + [sds(1, lev) if carry else part],
        )
        r = call(
            rest_body,
            (scale, x0, x1, x2, eg, dd[0], dd[1], dd[2], ds, dn),
            [SM] + [VM] * 9,
            [row5(nf), row3(nf), row5(nf)] + ([] if carry else [part]),
        )
        return tuple(o[:3]), tuple(r[:3]), (o[3] if carry else (o[3], r[3]))

    def forward(state, v):
        x0, x1, state = fwd_first(state, v[1], v[2])
        x2, x3, eg = fwd_last(state, v[3], x0, x1)
        return (x0, x1, x2, x3), eg

    def norm(v):
        return call(norm_body, tuple(v), [VM] * 4, [part])[0]

    chains = []
    for nf, gg, dd, ds, dn in groups:
        state = tuple(
            call(turn_first_body, (gg[3], gg[2], w3, ra), [VM] * 4, state_of(nf, 3))
        )
        g3, g2, state = adj_mid(state, gg[2], gg[1], gg[0])
        g0, g1, state = adj_last(0, state, gg[0])
        g = (g0, g1, g2, g3)
        xs, eg = forward(state, g)
        state, fs, bg = turn(xs, eg, dd, ds, dn, sig_arr)
        z3, z2, state = adj_mid(state, fs[2], fs[1])
        z0, z1, state = adj_last(1, state, fs[0])
        z = (z0, z1, z2, z3)
        xs, eg = forward(state, z)
        chains.append((g, z, xs, eg, norm(g), bg, norm(z)))
    ins = [ch[4] for ch in chains] + [q for ch in chains for q in ch[5]]
    ins += [ch[6] for ch in chains]
    for ch, (_, _, dd, _, _) in zip(chains, groups):
        ins += list(ch[2]) + list(dd)
    row = call(
        functools.partial(sums_body, len(chains)), tuple(ins), [VM] * len(ins), [sds(1, lev)]
    )[0]
    row = call(add_body, (row, swap(row)), [VM] * 2, [sds(1, lev)], flops=1e5)[0]
    row = ring_sum(row, 1)
    states = []
    for ch, (nf, gg, dd, ds, dn) in zip(chains, groups):
        state, fs, row = turn(ch[2], ch[3], dd, ds, dn, one_arr, row)
        states.append((state, fs))
    row = ring_sum(row, 4)
    mids = []
    for state, fs in states:
        w3z, w2z, state, row = adj_mid(state, fs[2], fs[1], None, row)
        mids.append((w3z, w2z, state, fs))
    row = ring_sum(row, 16)
    weights = call(solve_body, (span, row), [SM, VM], [sds(1, lev)], flops=1e5)[0]

    def final(kind, *vecs):
        nf = vecs[0][0].shape[0]
        ins = (c_arr, weights) + tuple(x for v in vecs for x in v)
        shape = sds(2, nf, 3, half, lev)
        keep, send = call(
            functools.partial(final_body, kind),
            ins,
            [SM] + [VM] * (len(ins) - 1),
            [shape, shape],
        )
        return keep, swap(send)

    def join(parts):
        n = len(parts)
        ins = (c_arr,) + tuple(p[0] for p in parts) + tuple(p[1] for p in parts)
        return call(
            functools.partial(join_body, half, n),
            ins,
            [SM] + [VM] * (2 * n),
            [sds(2, 1, FIELDS, 3, cols, lev)],
            scratch=[pltpu.SemaphoreType.DMA((4 * n,))],
            out_specs=[pl.BlockSpec(memory_space=pl.ANY)],
        )[0]

    increment = join([final("inc", ch[0], ch[1]) for ch in chains])
    ends = []
    for ch, (w3z, w2z, state, fs) in zip(chains, mids):
        w0z, w1z, _ = adj_last(2, state, fs[0])
        ends.append(final("res", ch[0], ch[1], (w0z, w1z, w2z, w3z)))
    return increment, join(ends)


def solution(mesh):
    in_specs = (
        P("tm", "space", None, None, None, None),
        P(),
        P("tm", "space", None, None, None),
        P("tm", "space", None, None, None),
        P("tm", "space", None, None),
        P("tm", "space", None, None),
        P("tm", "space", None),
    )
    out_specs = (P("tm", "space", None, None, None, None), P("tm", "space", None, None, None, None))
    return jax.shard_map(
        per_device, mesh=mesh, in_specs=in_specs, out_specs=out_specs, check_vma=False
    )
```

```python
import functools
import jax
import jax.numpy as jnp
from jax import lax
from jax.experimental import pallas as pl
from jax.experimental.pallas import tpu as pltpu
from jax.sharding import PartitionSpec as P

FIELDS = 3
MIXC = 0.25
SCALE_Q = 0.5
GROUPS = (FIELDS,)
PAD = 8
F32 = jnp.float32
BF16 = jnp.bfloat16

VM = pl.BlockSpec(memory_space=pltpu.VMEM)
SM = pl.BlockSpec(memory_space=pltpu.SMEM)


def call(body, ins, specs, outs, vmem=None, flops=1e8, scratch=(), out_specs=None):
    nbytes = sum(a.size * a.dtype.itemsize for a in ins)
    nbytes += sum(o.size * o.dtype.itemsize for o in outs)
    return pl.pallas_call(
        body,
        out_shape=outs,
        in_specs=specs,
        out_specs=out_specs or [VM] * len(outs),
        scratch_shapes=list(scratch),
        compiler_params=pltpu.CompilerParams(vmem_limit_bytes=vmem or 6 * 2**20),
        cost_estimate=pl.CostEstimate(
            flops=int(flops), bytes_accessed=int(nbytes), transcendentals=0
        ),
    )(*ins)


def sds(*shape, dtype=F32):
    return jax.ShapeDtypeStruct(shape, dtype)


def later(x):
    return pltpu.roll(x, 1, 0)


def earlier(x):
    return pltpu.roll(x, x.shape[0] - 1, 0)


def coef(w_ref, i):
    a = w_ref[0, i]
    b = w_ref[1, i]
    ap = jnp.maximum(a, 0.0)
    am = ap - a
    bp = jnp.maximum(b, 0.0)
    bm = bp - b
    return ap, am, bp, bm, 1.0 - (ap + am) - (bp + bm)


def mixed(v, rhs):
    lev = v.shape[1]
    hi = v.astype(BF16)
    lo = (v - hi.astype(F32)).astype(BF16)
    o = jnp.dot(jnp.concatenate([hi, lo], axis=1), rhs, preferred_element_type=F32)
    return v + (o[:, :lev] + o[:, lev:])


class Sides:

    def __init__(self, flag, first, second):
        self.even = flag > 0.5
        self.refs = (first, second)

    def south(self, k, f):
        return jnp.where(self.even, self.refs[1][k, f], self.refs[0][k, f])

    def north(self, k, f):
        return jnp.where(self.even, self.refs[0][k, f], self.refs[1][k, f])

    def put(self, k, f, south, north):
        self.refs[0][k, f] = jnp.where(self.even, north, south)
        self.refs[1][k, f] = jnp.where(self.even, south, north)


def adj_local(w, c):
    ap, am, _, _, c0 = c
    return c0 * w + earlier(ap * w) + later(am * w)


def fwd_local(u, c):
    ap, am, _, _, c0 = c
    return c0 * u + ap * later(u) + am * earlier(u)


def adj_pre(f, rows, w_ref, rhs, mid_ref, out):
    w = [mixed(x, rhs) for x in rows]
    c = [coef(w_ref, i) for i in range(3)]
    mid_ref[f] = adj_local(w[1], c[1]) + c[2][2] * w[2] + c[0][3] * w[0]
    out.put(
        0,
        f,
        adj_local(w[0], c[0]) + c[1][2] * w[1],
        adj_local(w[2], c[2]) + c[1][3] * w[1],
    )
    out.put(1, f, c[0][2] * w[0], c[2][3] * w[2])


def adj_post(f, mid_ref, own, got, fs, fn):
    return [
        (got.south(0, f) + own.south(1, f)) * fs,
        own.south(0, f) + got.south(1, f) * fs,
        mid_ref[f],
        own.north(0, f) + got.north(1, f) * fn,
        (got.north(0, f) + own.north(1, f)) * fn,
    ]


def adj_second(rows5, w_ref, wh_ref, rhs):
    w = [mixed(x, rhs) for x in rows5]
    c = [coef(w_ref, i) for i in range(3)]
    up = [c[1][2], c[2][2], wh_ref[1]]
    down = [wh_ref[0], c[0][3], c[1][3]]
    return [
        adj_local(w[i + 1], c[i]) + up[i] * w[i + 2] + down[i] * w[i] for i in range(3)
    ]


def fwd_pre(f, u, w_ref, mid_ref, out):
    c = [coef(w_ref, i) for i in range(3)]
    mid_ref[f] = fwd_local(u[1], c[1]) + c[1][2] * u[0] + c[1][3] * u[2]
    out.put(0, f, u[0], u[2])
    out.put(
        1,
        f,
        fwd_local(u[0], c[0]) + c[0][3] * u[1],
        fwd_local(u[2], c[2]) + c[2][2] * u[1],
    )


def fwd_post(f, mid_ref, own, got, w_ref, wh_ref, fs, fn, rhs):
    b0 = w_ref[1, 0]
    b2 = w_ref[1, 2]
    m = [
        got.south(1, f) * fs + wh_ref[0] * own.south(0, f),
        own.south(1, f) + jnp.maximum(b0, 0.0) * (got.south(0, f) * fs),
        mid_ref[f],
        own.north(1, f) + jnp.maximum(-b2, 0.0) * (got.north(0, f) * fn),
        got.north(1, f) * fn + wh_ref[1] * own.north(0, f),
    ]
    return [mixed(x, rhs) for x in m]


def fwd_second(u5, w_ref, rhs):
    out = []
    for i in range(3):
        c = coef(w_ref, i)
        m = fwd_local(u5[i + 1], c) + c[2] * u5[i] + c[3] * u5[i + 2]
        out.append(mixed(m, rhs))
    return out


def fields(n, body):
    if n == 1:
        body(0)
        return

    def step(f, carry):
        body(f)
        return carry

    lax.fori_loop(0, n, step, 0)


def fold(x):
    own = x[PAD:-PAD]
    return jnp.sum(own.reshape(own.shape[0] // 8, 8, own.shape[1]), axis=0)


def split_store(x, half, c, own_ref, snd_ref, idx):
    n = x.shape[0]
    low = jnp.concatenate([x[n - PAD :], x[: half + PAD]], axis=0)
    high = jnp.concatenate([x[half - PAD :], x[:PAD]], axis=0)

    @pl.when(c == 0)
    def _():
        own_ref[idx] = low
        snd_ref[idx] = high

    @pl.when(c != 0)
    def _():
        own_ref[idx] = high
        snd_ref[idx] = low


def pack_body(w_ref, d_ref, i_ref, o_ref, t_ref):
    t_ref[...] = jnp.zeros_like(t_ref)
    lev = o_ref.shape[-1]
    live = i_ref[...] >= 0.0
    for f in range(FIELDS):
        w = jnp.where(live, w_ref[:, :, f * lev : (f + 1) * lev], 0.0)
        o_ref[:, f] = w
        o_ref[:, FIELDS + f] = w * d_ref[:, :, f * lev : (f + 1) * lev]
    o_ref[:, 2 * FIELDS] = i_ref[...]


def emit(half, c, acc, at, own_ref, snd_ref):
    cols = 2 * half
    for w in range(2):

        def one(i, carry):
            base = (w * 3 + i) * (cols * 8) + at
            for f in range(FIELDS):
                x = acc[pl.ds(base + f, cols, stride=8), :]
                split_store(x, half, c, own_ref, snd_ref, (w, f, i))
            return carry

        lax.fori_loop(0, 3, one, 0)


def scatter_body(half, slots, c_ref, p_ref, acc, go_ref, gs_ref, idx_v, idx_s, sem):
    blocks = 2 * FIELDS + 1
    owners = p_ref.shape[0] // (blocks * slots)
    lev = p_ref.shape[1]
    lane = lanes((slots, lev))

    def column(o, vals):
        at = pl.multiple_of((o * blocks + blocks - 1) * slots, slots)
        return jnp.where(lane == o, p_ref[pl.ds(at, slots), :], vals)

    vals = lax.fori_loop(0, owners, column, jnp.zeros((slots, lev), F32))
    idx_v[...] = jnp.maximum(vals, 0.0).astype(jnp.int32)
    copy = pltpu.make_async_copy(idx_v, idx_s, sem)
    copy.start()
    cells = acc.shape[0] // 8
    chunk = 64

    def clear(t, carry):
        acc[pl.ds(pl.multiple_of(t * (8 * chunk), 8 * chunk), 8 * chunk), :] = jnp.zeros(
            (8 * chunk, lev), F32
        )
        return carry

    lax.fori_loop(0, cells // chunk, clear, 0)

    copy.wait()

    def put(o, carry):
        for s in range(slots):
            row = pl.multiple_of(idx_s[s, o] * 8, 8)
            x = p_ref[pl.ds(o * (blocks * slots) + s, blocks, stride=slots), :]
            acc[pl.ds(row, blocks), :] += x
        return carry

    lax.fori_loop(0, owners, put, 0)
    emit(half, c_ref[0], acc, FIELDS, go_ref, gs_ref)


def diag_body(half, c_ref, acc, do_ref, ds_ref):
    emit(half, c_ref[0], acc, 0, do_ref, ds_ref)


def wind_body(half, c_ref, w_ref, m_ref, t_ref, o_ref, s_ref, ra_ref, rf_ref):
    c = c_ref[0]
    for w in range(2):

        def one(i, carry):
            for k in range(2):
                split_store(w_ref[w, k, i].astype(F32), half, c, o_ref, s_ref, (w, k, i))
            return carry

        lax.fori_loop(0, 3, one, 0)
    for m, ref in ((m_ref[...] * MIXC, ra_ref), (m_ref[...].T * MIXC, rf_ref)):
        hi = m.astype(BF16)
        lo = (m - hi.astype(F32)).astype(BF16)
        line = jnp.concatenate([hi, lo], axis=1)
        ref[...] = jnp.concatenate([line, line], axis=0)


def pick_body(f0, c_ref, own_ref, got_ref, *outs):
    c = c_ref[0]
    nf = outs[0].shape[0]

    def put(src, dst):
        for w in range(2):
            for f in range(nf):
                dst[w][f] = src[w, f0 + f]

    @pl.when(c == 0)
    def _():
        put(own_ref, outs[:2])
        put(got_ref, outs[2:4])

    @pl.when(c != 0)
    def _():
        put(got_ref, outs[:2])
        put(own_ref, outs[2:4])


def pick_wind_body(c_ref, own_ref, got_ref, w0, w1, w2, w3, ss, sn):
    pick_body(0, c_ref, own_ref, got_ref, w0, w1, w2, w3)
    for k, w in enumerate((w0, w2)):
        ss[k] = jnp.maximum(w[1, 0], 0.0)
        sn[k] = jnp.maximum(-w[1, 2], 0.0)


def turn_first_body(fl, g3_ref, g2_ref, w3_ref, ra_ref, mid_ref, ss_ref, sn_ref):
    rhs = ra_ref[...]
    out = Sides(fl[2], ss_ref, sn_ref)

    def one(f):
        adj_pre(f, [g3_ref[f, i] for i in range(3)], w3_ref, rhs, mid_ref, out)
        out.put(2, f, g2_ref[f, 0], g2_ref[f, 2])

    fields(g3_ref.shape[0], one)


def five(f, f_ref, got, ext):
    if ext:
        return [got.south(2, f)] + [f_ref[f, i] for i in range(3)] + [got.north(2, f)]
    return [f_ref[f, i] for i in range(5)]


def adj_mid_body(ext, carry, *refs):
    if carry:
        refs[-1][...] = refs[12][...]
        refs = refs[:12] + refs[13:-1]
    (fl, mid, ss, sn, rs, rn, f2, f1, w2, wh2, w1, ra) = refs[:12]
    n = 12
    if ext:
        g0 = refs[n]
        n += 1
    g3, g2, mid_o, ss_o, sn_o = refs[n:]
    fs, fn = fl[0], fl[1]
    rhs = ra[...]
    own, got, out_o = Sides(fl[2], ss, sn), Sides(fl[2], rs, rn), Sides(fl[2], ss_o, sn_o)

    def one(f):
        lam = adj_post(f, mid, own, got, fs, fn)
        for i in range(5):
            g3[f, i] = lam[i] * SCALE_Q
        src = five(f, f2, got, ext)
        out = adj_second([lam[i] + src[i] for i in range(5)], w2, wh2, rhs)
        for i in range(3):
            g2[f, i] = out[i] * SCALE_Q
        adj_pre(f, [out[i] + f1[f, i] for i in range(3)], w1, rhs, mid_o, out_o)
        if ext:
            out_o.put(2, f, g0[f, 0], g0[f, 2])

    fields(mid.shape[0], one)


def adj_last_body(mode, *refs):
    (fl, mid, ss, sn, rs, rn, f0, w0, wh0, ra) = refs[:10]
    n = 10
    if mode == 0:
        d2 = refs[n]
        n += 1
    outs = refs[n:]
    fs, fn = fl[0], fl[1]
    rhs = ra[...]
    own, got = Sides(fl[2], ss, sn), Sides(fl[2], rs, rn)
    if mode < 2:
        out_o = Sides(fl[2], outs[3], outs[4])

    def one(f):
        lam = adj_post(f, mid, own, got, fs, fn)
        src = five(f, f0, got, mode == 0)
        out = adj_second([lam[i] + src[i] for i in range(5)], w0, wh0, rhs)
        for i in range(5):
            outs[1][f, i] = lam[i] * SCALE_Q
        for i in range(3):
            outs[0][f, i] = out[i]
        if mode < 2:
            fwd_pre(f, out, w0, outs[2], out_o)
        if mode == 0:
            out_o.put(2, f, d2[f, 0], d2[f, 2])

    fields(mid.shape[0], one)


def fwd_first_body(ride, fl, mid, ss, sn, rs, rn, v1, v2, w0, wh0, w1, w2, rf, *outs):
    if ride:
        d0, outs, halo = outs[0], outs[1:6], outs[6]
    x0, x1, mid_o, ss_o, sn_o = outs
    fs, fn = fl[0], fl[1]
    rhs = rf[...]
    own, got, out_o = Sides(fl[2], ss, sn), Sides(fl[2], rs, rn), Sides(fl[2], ss_o, sn_o)

    def one(f):
        x5 = fwd_post(f, mid, own, got, w0, wh0, fs, fn, rhs)
        for i in range(5):
            x0[f, i] = x5[i]
        x3 = fwd_second([x5[i] + SCALE_Q * v1[f, i] for i in range(5)], w1, rhs)
        for i in range(3):
            x1[f, i] = x3[i]
        fwd_pre(f, [x3[i] + SCALE_Q * v2[f, i] for i in range(3)], w2, mid_o, out_o)
        if ride:
            out_o.put(2, f, d0[f, 0], d0[f, 2])
            halo[0, f] = got.south(2, f)
            halo[1, f] = got.north(2, f)

    fields(mid.shape[0], one)


def edge(x, half):
    return jnp.concatenate([x[half : half + PAD], x[PAD : 2 * PAD]], axis=0)


def fwd_last_body(half, fl, mid, ss, sn, rs, rn, v3, x0, x1, w2, wh2, w3, rf, *outs):
    x2, x3, eg = outs[:3]
    fs, fn = fl[0], fl[1]
    rhs = rf[...]
    own, got = Sides(fl[2], ss, sn), Sides(fl[2], rs, rn)

    def one(f):
        x5 = fwd_post(f, mid, own, got, w2, wh2, fs, fn, rhs)
        for i in range(5):
            x2[f, i] = x5[i]
            eg[f, 8 + i] = edge(x5[i], half)
            eg[f, i] = edge(x0[f, i], half)
        y3 = fwd_second([x5[i] + SCALE_Q * v3[f, i] for i in range(5)], w3, rhs)
        for i in range(3):
            x3[f, i] = y3[i]
            eg[f, 13 + i] = edge(y3[i], half)
            eg[f, 5 + i] = edge(x1[f, i], half)
        if len(outs) > 3:
            outs[3][0, f] = got.south(2, f)
            outs[3][1, f] = got.north(2, f)

    fields(mid.shape[0], one)


def fixed(x, e):
    return jnp.concatenate([e[:PAD], x[PAD:-PAD], e[PAD:]], axis=0)


def turn_body(carry, fl, sc, x3, eg, d3, w3, ra, *outs):
    if carry:
        outs[4][...] = outs[0][...]
        outs = outs[1:4]
    mid, ss, sn = outs[:3]
    q = None if carry else outs[3]
    out = Sides(fl[2], ss, sn)
    rhs = ra[...]
    if q is not None:
        q[...] = jnp.zeros_like(q)
    scale = sc[0]

    def one(f):
        rows = []
        for i in range(3):
            y = fixed(x3[f, i], eg[f, 13 + i])
            t = d3[f, i] * y
            if q is not None:
                q[...] += fold(t * y)
            rows.append(t * scale)
        adj_pre(f, rows, w3, rhs, mid, out)

    fields(x3.shape[0], one)


def rest_body(sc, x0, x1, x2, eg, d0, d1, d2, h0, h2, f0, f1, f2, q=None):
    if q is not None:
        q[...] = jnp.zeros_like(q)
    scale = sc[0]

    def one(f):
        for x, rows, at, d, h, f_o in (
            (x0, 5, 0, d0, h0, f0),
            (x1, 3, 5, d1, None, f1),
            (x2, 5, 8, d2, h2, f2),
        ):
            for i in range(rows):
                y = fixed(x[f, i], eg[f, at + i])
                if rows == 5 and i == 0:
                    t = h[0, f] * y
                elif rows == 5 and i == 4:
                    t = h[1, f] * y
                else:
                    t = d[f, i - (rows == 5)] * y
                    if q is not None:
                        q[...] += fold(t * y)
                f_o[f, i] = t * scale

    fields(x0.shape[0], one)


def norm_body(v0, v1, v2, v3, q):
    q[...] = jnp.zeros_like(q)

    def one(f):
        for v, off in ((v0, 0), (v1, 1), (v2, 0), (v3, 1)):
            for i in range(3):
                x = v[f, i + off]
                q[...] += fold(x * x)

    fields(v0.shape[0], one)


def lanes(shape):
    return lax.broadcasted_iota(jnp.int32, shape, len(shape) - 1)


def sums_body(n, *refs):
    out = refs[-1]
    parts = [refs[:n], refs[n : 3 * n], refs[3 * n : 4 * n]]
    acc = jnp.zeros(refs[0].shape, F32)
    at = 4 * n
    for _ in range(n):
        xs, ds = refs[at : at + 4], refs[at + 4 : at + 8]
        at += 8

        def one(f, acc):
            for x, d in zip(xs, ds):
                off = (x.shape[1] - 3) // 2
                for i in range(3):
                    v = x[f, i + off]
                    acc = acc + fold(d[f, i] * v * v)
            return acc

        nf = xs[0].shape[0]
        acc = one(0, acc) if nf == 1 else lax.fori_loop(0, nf, one, acc)
    lane = lanes(out.shape)
    row = jnp.where(lane == 3, jnp.sum(acc, keepdims=True), 0.0)
    for k in range(3):
        val = parts[k][0][...]
        for p in parts[k][1:]:
            val = val + p[...]
        row = jnp.where(lane == k, jnp.sum(val, keepdims=True), row)
    out[...] = row


def add_body(a, b, out):
    out[...] = a[...] + b[...]


def ring_body(step, pos_ref, a, b, c, d, out):
    mine = lax.rem(lax.div(pos_ref[0], step), 4)
    rows = [a[...], b[...], c[...], d[...]]
    total = jnp.zeros(out.shape, F32)
    for place in range(4):
        gap = lax.rem(mine + 4 - place, 4)
        term = rows[0]
        for k in (1, 2, 3):
            term = jnp.where(gap == k, rows[k], term)
        total = total + term
    out[...] = total


def solve_body(hs, got, out):
    row = got[...]
    at = lanes(row.shape)

    def pick(k):
        return jnp.sum(jnp.where(at == k, row, 0.0), axis=1, keepdims=True)

    rr, bg, zz, bz = [pick(k) for k in range(4)]
    sig, inv = hs[0], hs[1]
    a0 = rr / (rr + bg)
    left = bg / (rr + bg)
    c = a0 * inv
    sbg = bg * sig
    rr1 = c * (c * (zz - sbg * (sbg / rr)))
    beta = rr1 / rr
    p = left + beta
    curve = p * (p * bg) - 2.0 * (p * (c * (inv * zz))) + c * (c * bz)
    a1 = rr1 / (rr1 + beta * beta * rr + curve)
    terms = (
        a0 + a1 * p,
        -(a1 * c),
        left - a1 * p,
        a1 * c - c - a1 * (p * inv),
        a1 * c,
    )
    w = jnp.zeros(row.shape, F32)
    for k, t in enumerate(terms):
        w = jnp.where(at == k, t, w)
    out[...] = w


def outbound_body(c_ref, v0, v1, v2, v3, out):
    v = (v0, v1, v2, v3)

    def put(first):
        for k in (first, first + 1):
            off = k % 2
            for f in range(out.shape[1]):
                for i in range(3):
                    out[k % 2, f, i] = v[k][f, i + off][PAD:-PAD]

    @pl.when(c_ref[0] == 0)
    def _():
        put(2)

    @pl.when(c_ref[0] != 0)
    def _():
        put(0)


def final_body(half, c_ref, k_ref, *refs):
    g, z, w = refs[0:4], refs[4:8], refs[8:12]
    og, oz, ow = refs[12:15]
    inc, res, ib, rb, sem = refs[15:]
    row = k_ref[...]
    at = lanes(row.shape)
    ig, iz, rg, rz, rw = [
        jnp.sum(jnp.where(at == k, row, 0.0), axis=1, keepdims=True) for k in range(5)
    ]
    c = c_ref[0]
    nf = og.shape[1]

    def put(first, mine, theirs):
        copies = []
        for k in (first, first + 1):
            n, off = k % 2, k % 2
            for f in range(nf):
                for i in range(3):
                    x = [v[k][f, i + off][PAD:-PAD] for v in (g, z, w)]
                    y = [v[n, f, i] for v in (og, oz, ow)]
                    for (a, b, d), lo in ((x, mine), (y, theirs)):
                        ib[n, f, i, lo : lo + half] = ig * a + iz * b
                        rb[n, f, i, lo : lo + half] = rg * a + rz * b + rw * d
                for src, dst in ((ib, inc), (rb, res)):
                    copy = pltpu.make_async_copy(
                        src.at[n, f], dst.at[n, 0, f], sem.at[len(copies)]
                    )
                    copy.start()
                    copies.append(copy)
        for copy in copies:
            copy.wait()

    @pl.when(c == 0)
    def _():
        put(0, 0, half)

    @pl.when(c != 0)
    def _():
        put(2, half, 0)


def per_device(winds, mixing, innovations, obs_weight, obs_sub, obs_col, obs_count):
    owners, slots = obs_sub.shape[2], obs_sub.shape[3]
    lev = mixing.shape[0]
    cols = winds.shape[4]
    half = cols // 2
    wide = half + 2 * PAD
    cells = winds.shape[3] * cols
    c = lax.axis_index("tm").astype(jnp.int32)
    pos = lax.axis_index("space")
    bands = lax.axis_size("space")
    c_arr = c.reshape(1)
    pos_arr = pos.astype(jnp.int32).reshape(1)
    even = pos % 2 == 0
    flags = jnp.stack([pos > 0, pos < bands - 1, even]).astype(F32)
    first_pairs = [(i, i ^ 1) for i in range(bands)]
    second_pairs = [(i, (((i + 1) ^ 1) - 1) % bands) for i in range(bands)]

    def swap(x):
        return lax.ppermute(x, "tm", [(0, 1), (1, 0)])

    def exchange(a, b):
        return lax.ppermute(a, "space", first_pairs), lax.ppermute(b, "space", second_pairs)

    def ring_sum(row, step):
        shifts = []
        for k in (1, 2, 3):
            pairs = []
            for i in range(bands):
                digit = (i // step) % 4
                pairs.append((i, i + ((digit + k) % 4 - digit) * step))
            shifts.append(pairs)
        got = tuple(lax.ppermute(row, "space", p) for p in shifts)
        return call(
            functools.partial(ring_body, step),
            (pos_arr, row) + got,
            [SM] + [VM] * 4,
            [sds(1, lev)],
            flops=1e5,
        )[0]

    live = (
        jnp.arange(slots, dtype=jnp.int32)[None, :] < obs_count.reshape(owners)[:, None]
    )
    place = (obs_sub * cells + obs_col).reshape(owners, slots)
    place = jnp.where(live, place, -1).astype(F32)
    place = jnp.broadcast_to(place[..., None], (owners, slots, lev))
    blocks = 2 * FIELDS + 1
    packed, token = call(
        pack_body,
        (
            obs_weight.reshape(owners, slots, -1),
            innovations.reshape(owners, slots, -1),
            place,
        ),
        [VM] * 3,
        [sds(owners, blocks, slots, lev), sds(8, lev)],
    )
    got = lax.all_to_all(packed, "space", split_axis=0, concat_axis=0, tiled=True)

    w_own, w_snd, ra, rf = call(
        functools.partial(wind_body, half),
        (c_arr, winds[:, 0], mixing, token),
        [SM] + [VM] * 3,
        [sds(2, 2, 3, wide, lev)] * 2 + [sds(2 * lev, 2 * lev, dtype=BF16)] * 2,
    )
    w_got = swap(w_snd)
    w0, w1, w2, w3, down, up = call(
        pick_wind_body,
        (c_arr, w_own, w_got),
        [SM, VM, VM],
        [sds(2, 3, wide, lev)] * 4 + [sds(2, wide, lev)] * 2,
    )
    one_side, other_side = exchange(jnp.where(even, up, down), jnp.where(even, down, up))
    from_s = jnp.where(pos > 0, jnp.where(even, other_side, one_side), 0.0)
    from_n = jnp.where(pos < bands - 1, jnp.where(even, one_side, other_side), 0.0)
    wh0 = jnp.stack([from_s[0], from_n[0]])
    wh2 = jnp.stack([from_s[1], from_n[1]])

    size = jnp.abs(mixing)
    grow = (1.0 + MIXC * jnp.max(jnp.sum(size, 0))) * (1.0 + MIXC * jnp.max(jnp.sum(size, 1)))
    grow = grow * grow
    inv = grow * grow
    sig = 1.0 / inv
    sig_arr = sig.reshape(1)
    one_arr = jnp.ones((1,), F32)
    span = jnp.stack([sig, 1.0 / sig])

    flat = got.reshape(owners * blocks * slots, lev)
    flat, wh0, wh2, w0, w1, w2, w3, sig_arr, span = lax.optimization_barrier(
        (flat, wh0, wh2, w0, w1, w2, w3, sig_arr, span)
    )
    halves = [sds(2, FIELDS, 3, wide, lev)] * 2
    acc, g_own, g_snd = call(
        functools.partial(scatter_body, half, slots),
        (c_arr, flat),
        [SM, VM],
        [sds(2 * cells * 8, lev)] + halves,
        scratch=[
            pltpu.VMEM((slots, lev), jnp.int32),
            pltpu.SMEM((slots, lev), jnp.int32),
            pltpu.SemaphoreType.DMA(()),
        ],
    )
    g_got = swap(g_snd)
    d_own, d_snd = call(functools.partial(diag_body, half), (c_arr, acc), [SM, VM], halves)
    d_got = swap(d_snd)
    groups = []
    f0 = 0
    for nf in GROUPS:
        shapes = [sds(nf, 3, wide, lev)] * 4
        pick = functools.partial(pick_body, f0)
        gg = call(pick, (c_arr, g_own, g_got), [SM, VM, VM], shapes)
        dd = call(pick, (c_arr, d_own, d_got), [SM, VM, VM], shapes)
        groups.append((nf, gg, dd))
        f0 += nf

    part = sds(8, lev)

    def row3(nf):
        return sds(nf, 3, wide, lev)

    def row5(nf):
        return sds(nf, 5, wide, lev)

    def state_of(nf, n):
        return [sds(nf, wide, lev)] + [sds(n, nf, wide, lev)] * 2

    def adj_mid(state, f2, f1, g0=None, row=None):
        mid, ss, sn = state
        nf = mid.shape[0]
        rs, rn = exchange(ss, sn)
        ext = g0 is not None
        carry = row is not None
        n = 3 if ext else 2
        ins = (flags, mid, ss, sn, rs, rn, f2, f1, w2, wh2, w1, ra) + ((g0,) if ext else ())
        ins += (row,) if carry else ()
        o = call(
            functools.partial(adj_mid_body, ext, carry),
            ins,
            [SM] + [VM] * (len(ins) - 1),
            [row5(nf), row3(nf)] + state_of(nf, n) + ([sds(1, lev)] if carry else []),
        )
        if carry:
            return o[0], o[1], tuple(o[2:5]), o[5]
        return o[0], o[1], tuple(o[2:])

    def adj_last(mode, state, f0, ride=()):
        mid, ss, sn = state
        nf = mid.shape[0]
        rs, rn = exchange(ss, sn)
        ins = (flags, mid, ss, sn, rs, rn, f0, w0, wh0, ra) + tuple(ride)
        specs = [SM] + [VM] * (len(ins) - 1)
        outs = [row3(nf), row5(nf)]
        outs += state_of(nf, 3 if mode == 0 else 2) if mode < 2 else []
        o = call(functools.partial(adj_last_body, mode), ins, specs, outs)
        return o[0], o[1], tuple(o[2:])

    def fwd_first(state, v1, v2, ride=()):
        mid, ss, sn = state
        nf = mid.shape[0]
        rs, rn = exchange(ss, sn)
        ins = (flags, mid, ss, sn, rs, rn, v1, v2, w0, wh0, w1, w2, rf) + ride
        o = call(
            functools.partial(fwd_first_body, len(ride) > 0),
            ins,
            [SM] + [VM] * (len(ins) - 1),
            [row5(nf), row3(nf)]
            + state_of(nf, 3 if ride else 2)
            + ([sds(2, nf, wide, lev)] if ride else []),
        )
        return o[0], o[1], tuple(o[2:5]), o[5:]

    def fwd_last(state, v3, x0, x1, ride):
        mid, ss, sn = state
        nf = mid.shape[0]
        rs, rn = exchange(ss, sn)
        ins = (flags, mid, ss, sn, rs, rn, v3, x0, x1, w2, wh2, w3, rf)
        return call(
            functools.partial(fwd_last_body, half),
            ins,
            [SM] + [VM] * 12,
            [row5(nf), row3(nf), sds(nf, 16, 2 * PAD, lev)]
            + ([sds(2, nf, wide, lev)] if ride else []),
        )

    def turn(xs, eg, dd, halo, scale, row=None):
        eg = swap(eg)
        x0, x1, x2, x3 = xs
        nf = x3.shape[0]
        carry = row is not None
        o = call(
            functools.partial(turn_body, carry),
            (flags, scale, x3, eg, dd[3], w3, ra) + ((row,) if carry else ()),
            [SM] * 2 + [VM] * (6 if carry else 5),
            state_of(nf, 2) + [sds(1, lev) if carry else part],
        )
        r = call(
            rest_body,
            (scale, x0, x1, x2, eg, dd[0], dd[1], dd[2]) + halo,
            [SM] + [VM] * 9,
            [row5(nf), row3(nf), row5(nf)] + ([] if carry else [part]),
        )
        return tuple(o[:3]), tuple(r[:3]), (o[3] if carry else (o[3], r[3]))

    def forward(state, v, ride=()):
        x0, x1, state, halo2 = fwd_first(state, v[1], v[2], ride)
        o = fwd_last(state, v[3], x0, x1, len(ride) > 0)
        return (x0, x1) + tuple(o[:2]), o[2], tuple(o[3:]) + tuple(halo2)

    def norm(v):
        return call(norm_body, tuple(v), [VM] * 4, [part])[0]

    chains = []
    for nf, gg, dd in groups:
        state = tuple(
            call(
                turn_first_body,
                (flags, gg[3], gg[2], w3, ra),
                [SM] + [VM] * 4,
                state_of(nf, 3),
            )
        )
        g3, g2, state = adj_mid(state, gg[2], gg[1], gg[0])
        g0, g1, state = adj_last(0, state, gg[0], (dd[2],))
        g = (g0, g1, g2, g3)
        xs, eg, halo = forward(state, g, (dd[0],))
        state, fs, bg = turn(xs, eg, dd, halo, sig_arr)
        z3, z2, state = adj_mid(state, fs[2], fs[1])
        z0, z1, state = adj_last(1, state, fs[0])
        z = (z0, z1, z2, z3)
        xs, eg, _ = forward(state, z)
        chains.append((g, z, xs, eg, norm(g), bg, norm(z), halo))
    ins = [ch[4] for ch in chains] + [q for ch in chains for q in ch[5]]
    ins += [ch[6] for ch in chains]
    for ch, (_, _, dd) in zip(chains, groups):
        ins += list(ch[2]) + list(dd)
    row = call(
        functools.partial(sums_body, len(chains)), tuple(ins), [VM] * len(ins), [sds(1, lev)]
    )[0]
    row = call(add_body, (row, swap(row)), [VM] * 2, [sds(1, lev)], flops=1e5)[0]
    states = []
    for ch, (nf, gg, dd) in zip(chains, groups):
        state, fs, row = turn(ch[2], ch[3], dd, ch[7], one_arr, row)
        states.append((state, fs))
    row = ring_sum(ring_sum(row, 1), 4)
    mids = []
    for state, fs in states:
        w3z, w2z, state, row = adj_mid(state, fs[2], fs[1], None, row)
        mids.append((w3z, w2z, state, fs))
    row = ring_sum(row, 16)
    weights = call(solve_body, (span, row), [SM, VM], [sds(1, lev)], flops=1e5)[0]

    g, z = chains[0][0], chains[0][1]
    w3z, w2z, state, fs = mids[0]
    w0z, w1z, _ = adj_last(2, state, fs[0])
    w = (w0z, w1z, w2z, w3z)
    shape = sds(2, FIELDS, 3, half, lev)

    def other(v):
        return swap(
            call(outbound_body, (c_arr,) + tuple(v), [SM] + [VM] * 4, [shape])[0]
        )

    ins = (c_arr, weights) + tuple(g) + tuple(z) + w + (other(g), other(z), other(w))
    full = (2, FIELDS, 3, cols, lev)
    return call(
        functools.partial(final_body, half),
        ins,
        [SM] + [VM] * (len(ins) - 1),
        [sds(2, 1, FIELDS, 3, cols, lev)] * 2,
        scratch=[
            pltpu.VMEM(full, F32),
            pltpu.VMEM(full, F32),
            pltpu.SemaphoreType.DMA((4 * FIELDS,)),
        ],
        out_specs=[pl.BlockSpec(memory_space=pl.ANY)] * 2,
        vmem=12 * 2**20,
    )


def solution(mesh):
    in_specs = (
        P("tm", "space", None, None, None, None),
        P(),
        P("tm", "space", None, None, None),
        P("tm", "space", None, None, None),
        P("tm", "space", None, None),
        P("tm", "space", None, None),
        P("tm", "space", None),
    )
    out_specs = (P("tm", "space", None, None, None, None), P("tm", "space", None, None, None, None))
    return jax.shard_map(
        per_device, mesh=mesh, in_specs=in_specs, out_specs=out_specs, check_vma=False
    )
```

```python
import functools
import jax
import jax.numpy as jnp
from jax import lax
from jax.experimental import pallas as pl
from jax.experimental.pallas import tpu as pltpu
from jax.sharding import PartitionSpec as P

FIELDS = 3
MIXC = 0.25
SCALE_Q = 0.5
GROUPS = (FIELDS,)
PAD = 8
F32 = jnp.float32
BF16 = jnp.bfloat16

VM = pl.BlockSpec(memory_space=pltpu.VMEM)
SM = pl.BlockSpec(memory_space=pltpu.SMEM)


def call(body, ins, specs, outs, vmem=None, flops=1e8, scratch=(), out_specs=None):
    nbytes = sum(a.size * a.dtype.itemsize for a in ins)
    nbytes += sum(o.size * o.dtype.itemsize for o in outs)
    return pl.pallas_call(
        body,
        out_shape=outs,
        in_specs=specs,
        out_specs=out_specs or [VM] * len(outs),
        scratch_shapes=list(scratch),
        compiler_params=pltpu.CompilerParams(vmem_limit_bytes=vmem or 6 * 2**20),
        cost_estimate=pl.CostEstimate(
            flops=int(flops), bytes_accessed=int(nbytes), transcendentals=0
        ),
    )(*ins)


def sds(*shape, dtype=F32):
    return jax.ShapeDtypeStruct(shape, dtype)


def later(x):
    return pltpu.roll(x, 1, 0)


def earlier(x):
    return pltpu.roll(x, x.shape[0] - 1, 0)


def coef(w_ref, i):
    a = w_ref[0, i]
    b = w_ref[1, i]
    ap = jnp.maximum(a, 0.0)
    am = ap - a
    bp = jnp.maximum(b, 0.0)
    bm = bp - b
    return ap, am, bp, bm, 1.0 - (ap + am) - (bp + bm)


def mixed(v, rhs):
    lev = v.shape[1]
    hi = v.astype(BF16)
    lo = (v - hi.astype(F32)).astype(BF16)
    o = jnp.dot(jnp.concatenate([hi, lo], axis=1), rhs, preferred_element_type=F32)
    return v + (o[:, :lev] + o[:, lev:])


class Sides:

    def __init__(self, flag, first, second):
        self.even = flag > 0.5
        self.refs = (first, second)

    def south(self, k, f):
        return jnp.where(self.even, self.refs[1][k, f], self.refs[0][k, f])

    def north(self, k, f):
        return jnp.where(self.even, self.refs[0][k, f], self.refs[1][k, f])

    def put(self, k, f, south, north):
        self.refs[0][k, f] = jnp.where(self.even, north, south)
        self.refs[1][k, f] = jnp.where(self.even, south, north)


def adj_local(w, c):
    ap, am, _, _, c0 = c
    return c0 * w + earlier(ap * w) + later(am * w)


def fwd_local(u, c):
    ap, am, _, _, c0 = c
    return c0 * u + ap * later(u) + am * earlier(u)


def adj_pre(f, rows, w_ref, ends, next_ref, rhs, mid_ref, pp_ref, out):
    w = [mixed(x, rhs) for x in rows]
    c = [coef(w_ref, i) for i in range(3)]
    low = adj_local(w[0], c[0]) + c[1][2] * w[1]
    high = adj_local(w[2], c[2]) + c[1][3] * w[1]
    mid_ref[f] = adj_local(w[1], c[1]) + c[2][2] * w[2] + c[0][3] * w[0]
    pp_ref[0, f] = low
    pp_ref[1, f] = high
    south = jnp.maximum(next_ref[1, 0], 0.0) * mixed(low + ends[0], rhs)
    north = jnp.maximum(-next_ref[1, 2], 0.0) * mixed(high + ends[1], rhs)
    out.put(0, f, south, north)
    out.put(1, f, c[0][2] * w[0], c[2][3] * w[2])


def adj_post(f, mid_ref, pp_ref, got, fs, fn):
    return [
        pp_ref[0, f] + got.south(1, f) * fs,
        mid_ref[f],
        pp_ref[1, f] + got.north(1, f) * fn,
    ]


def adj_second(f, rows, w_ref, wh_ref, rhs, own, got, fs, fn):
    w = [mixed(x, rhs) for x in rows]
    c = [coef(w_ref, i) for i in range(3)]
    below = got.south(0, f) * fs + wh_ref[0] * mixed(own.south(1, f), rhs)
    above = got.north(0, f) * fn + wh_ref[1] * mixed(own.north(1, f), rhs)
    return [
        adj_local(w[0], c[0]) + c[1][2] * w[1] + below,
        adj_local(w[1], c[1]) + c[2][2] * w[2] + c[0][3] * w[0],
        adj_local(w[2], c[2]) + c[1][3] * w[1] + above,
    ]


def fwd_pre(f, u, w_ref, ends, rhs, mid_ref, pp_ref, out):
    c = [coef(w_ref, i) for i in range(3)]
    low = fwd_local(u[0], c[0]) + c[0][3] * u[1]
    high = fwd_local(u[2], c[2]) + c[2][2] * u[1]
    mid_ref[f] = fwd_local(u[1], c[1]) + c[1][2] * u[0] + c[1][3] * u[2]
    pp_ref[0, f] = low
    pp_ref[1, f] = high
    out.put(0, f, u[0], u[2])
    out.put(1, f, mixed(low, rhs) + ends[0], mixed(high, rhs) + ends[1])


def fwd_post(f, mid_ref, pp_ref, own, got, w_ref, wh_ref, fs, fn, rhs):
    b0 = w_ref[1, 0]
    b2 = w_ref[1, 2]
    m = [
        pp_ref[0, f] + jnp.maximum(b0, 0.0) * (got.south(0, f) * fs),
        mid_ref[f],
        pp_ref[1, f] + jnp.maximum(-b2, 0.0) * (got.north(0, f) * fn),
    ]
    below = (got.south(1, f) + mixed(wh_ref[0] * own.south(0, f), rhs)) * fs
    above = (got.north(1, f) + mixed(wh_ref[1] * own.north(0, f), rhs)) * fn
    return [mixed(x, rhs) for x in m], below, above


def fwd_second(u5, w_ref, rhs):
    out = []
    for i in range(3):
        c = coef(w_ref, i)
        m = fwd_local(u5[i + 1], c) + c[2] * u5[i] + c[3] * u5[i + 2]
        out.append(mixed(m, rhs))
    return out


def fields(n, body):
    if n == 1:
        body(0)
        return

    def step(f, carry):
        body(f)
        return carry

    lax.fori_loop(0, n, step, 0)


def fold(x):
    own = x[PAD:-PAD]
    return jnp.sum(own.reshape(own.shape[0] // 8, 8, own.shape[1]), axis=0)


def split_store(x, half, c, own_ref, snd_ref, idx):
    n = x.shape[0]
    low = jnp.concatenate([x[n - PAD :], x[: half + PAD]], axis=0)
    high = jnp.concatenate([x[half - PAD :], x[:PAD]], axis=0)

    @pl.when(c == 0)
    def _():
        own_ref[idx] = low
        snd_ref[idx] = high

    @pl.when(c != 0)
    def _():
        own_ref[idx] = high
        snd_ref[idx] = low


def pack_body(w_ref, d_ref, i_ref, o_ref, t_ref):
    t_ref[...] = jnp.zeros_like(t_ref)
    lev = o_ref.shape[-1]
    live = i_ref[...] >= 0.0
    for f in range(FIELDS):
        w = jnp.where(live, w_ref[:, :, f * lev : (f + 1) * lev], 0.0)
        o_ref[:, f] = w
        o_ref[:, FIELDS + f] = w * d_ref[:, :, f * lev : (f + 1) * lev]
    o_ref[:, 2 * FIELDS] = i_ref[...]


def emit(half, c, acc, at, own_ref, snd_ref):
    cols = 2 * half
    for w in range(2):

        def one(i, carry):
            base = (w * 3 + i) * (cols * 8) + at
            for f in range(FIELDS):
                x = acc[pl.ds(base + f, cols, stride=8), :]
                split_store(x, half, c, own_ref, snd_ref, (w, f, i))
            return carry

        lax.fori_loop(0, 3, one, 0)


def scatter_body(half, slots, c_ref, p_ref, acc, go_ref, gs_ref, idx_v, idx_s, sem):
    blocks = 2 * FIELDS + 1
    owners = p_ref.shape[0] // (blocks * slots)
    lev = p_ref.shape[1]
    lane = lanes((slots, lev))

    def column(o, vals):
        at = pl.multiple_of((o * blocks + blocks - 1) * slots, slots)
        return jnp.where(lane == o, p_ref[pl.ds(at, slots), :], vals)

    vals = lax.fori_loop(0, owners, column, jnp.zeros((slots, lev), F32))
    idx_v[...] = jnp.maximum(vals, 0.0).astype(jnp.int32)
    copy = pltpu.make_async_copy(idx_v, idx_s, sem)
    copy.start()
    cells = acc.shape[0] // 8
    chunk = 64

    def clear(t, carry):
        acc[pl.ds(pl.multiple_of(t * (8 * chunk), 8 * chunk), 8 * chunk), :] = jnp.zeros(
            (8 * chunk, lev), F32
        )
        return carry

    lax.fori_loop(0, cells // chunk, clear, 0)

    copy.wait()

    def put(o, carry):
        for s in range(slots):
            row = pl.multiple_of(idx_s[s, o] * 8, 8)
            x = p_ref[pl.ds(o * (blocks * slots) + s, blocks, stride=slots), :]
            acc[pl.ds(row, blocks), :] += x
        return carry

    lax.fori_loop(0, owners, put, 0)
    emit(half, c_ref[0], acc, FIELDS, go_ref, gs_ref)


def diag_body(half, c_ref, acc, do_ref, ds_ref):
    emit(half, c_ref[0], acc, 0, do_ref, ds_ref)


def wind_body(half, c_ref, w_ref, m_ref, t_ref, o_ref, s_ref, ra_ref, rf_ref):
    c = c_ref[0]
    for w in range(2):

        def one(i, carry):
            for k in range(2):
                split_store(w_ref[w, k, i].astype(F32), half, c, o_ref, s_ref, (w, k, i))
            return carry

        lax.fori_loop(0, 3, one, 0)
    for m, ref in ((m_ref[...] * MIXC, ra_ref), (m_ref[...].T * MIXC, rf_ref)):
        hi = m.astype(BF16)
        lo = (m - hi.astype(F32)).astype(BF16)
        line = jnp.concatenate([hi, lo], axis=1)
        ref[...] = jnp.concatenate([line, line], axis=0)


def pick_body(f0, c_ref, own_ref, got_ref, *outs):
    c = c_ref[0]
    nf = outs[0].shape[0]

    def put(src, dst):
        for w in range(2):
            for f in range(nf):
                dst[w][f] = src[w, f0 + f]

    @pl.when(c == 0)
    def _():
        put(own_ref, outs[:2])
        put(got_ref, outs[2:4])

    @pl.when(c != 0)
    def _():
        put(got_ref, outs[:2])
        put(own_ref, outs[2:4])


def pick_wind_body(c_ref, own_ref, got_ref, w0, w1, w2, w3, ss, sn):
    pick_body(0, c_ref, own_ref, got_ref, w0, w1, w2, w3)
    for k, w in enumerate((w0, w2)):
        ss[k] = jnp.maximum(w[1, 0], 0.0)
        sn[k] = jnp.maximum(-w[1, 2], 0.0)


def turn_first_body(fl, g3, g2, w3, w2, ra, mid, pp, ss, sn):
    rhs = ra[...]
    out = Sides(fl[2], ss, sn)

    def one(f):
        rows = [g3[f, i] for i in range(3)]
        adj_pre(f, rows, w3, (g2[f, 0], g2[f, 2]), w2, rhs, mid, pp, out)

    fields(g3.shape[0], one)


def adj_mid_body(carry, *refs):
    if carry:
        refs[-1][...] = refs[15][...]
        refs = refs[:15] + refs[16:-1]
    (fl, mid, pp, ss, sn, rs, rn, f2, f1, f0, w2, wh2, w1, w0, ra) = refs[:15]
    g3, g2, mid_o, pp_o, ss_o, sn_o = refs[15:]
    fs, fn = fl[0], fl[1]
    rhs = ra[...]
    own, got, out_o = Sides(fl[2], ss, sn), Sides(fl[2], rs, rn), Sides(fl[2], ss_o, sn_o)

    def one(f):
        lam = adj_post(f, mid, pp, got, fs, fn)
        for i in range(3):
            g3[f, i] = lam[i] * SCALE_Q
        rows = [lam[i] + f2[f, i] for i in range(3)]
        out = adj_second(f, rows, w2, wh2, rhs, own, got, fs, fn)
        for i in range(3):
            g2[f, i] = out[i] * SCALE_Q
        rows = [out[i] + f1[f, i] for i in range(3)]
        adj_pre(f, rows, w1, (f0[f, 0], f0[f, 2]), w0, rhs, mid_o, pp_o, out_o)

    fields(mid.shape[0], one)


def adj_last_body(more, *refs):
    (fl, mid, pp, ss, sn, rs, rn, f0, w0, wh0, ra, rf) = refs[:12]
    outs = refs[12:]
    fs, fn = fl[0], fl[1]
    rhs = ra[...]
    own, got = Sides(fl[2], ss, sn), Sides(fl[2], rs, rn)
    if more:
        out_o = Sides(fl[2], outs[4], outs[5])

    def one(f):
        lam = adj_post(f, mid, pp, got, fs, fn)
        rows = [lam[i] + f0[f, i] for i in range(3)]
        out = adj_second(f, rows, w0, wh0, rhs, own, got, fs, fn)
        for i in range(3):
            outs[1][f, i] = lam[i] * SCALE_Q
            outs[0][f, i] = out[i]
        if more:
            half = SCALE_Q * SCALE_Q
            ends = (half * lam[0], half * lam[2])
            fwd_pre(f, out, w0, ends, rf[...], outs[2], outs[3], out_o)

    fields(mid.shape[0], one)


def fwd_first_body(fl, mid, pp, ss, sn, rs, rn, v1, v2, v3, w0, wh0, w1, w2, rf, *outs):
    x0, x1, mid_o, pp_o, ss_o, sn_o = outs
    fs, fn = fl[0], fl[1]
    rhs = rf[...]
    own, got, out_o = Sides(fl[2], ss, sn), Sides(fl[2], rs, rn), Sides(fl[2], ss_o, sn_o)

    def one(f):
        x, below, above = fwd_post(f, mid, pp, own, got, w0, wh0, fs, fn, rhs)
        for i in range(3):
            x0[f, i] = x[i]
        u = [x[i] + SCALE_Q * v1[f, i] for i in range(3)]
        x = fwd_second([below] + u + [above], w1, rhs)
        for i in range(3):
            x1[f, i] = x[i]
        u = [x[i] + SCALE_Q * v2[f, i] for i in range(3)]
        ends = (SCALE_Q * v3[f, 0], SCALE_Q * v3[f, 2])
        fwd_pre(f, u, w2, ends, rhs, mid_o, pp_o, out_o)

    fields(mid.shape[0], one)


def edge(x, half):
    return jnp.concatenate([x[half : half + PAD], x[PAD : 2 * PAD]], axis=0)


def fwd_last_body(half, fl, mid, pp, ss, sn, rs, rn, v3, x0, x1, w2, wh2, w3, rf, *outs):
    x2, x3, eg = outs
    fs, fn = fl[0], fl[1]
    rhs = rf[...]
    own, got = Sides(fl[2], ss, sn), Sides(fl[2], rs, rn)

    def one(f):
        x, below, above = fwd_post(f, mid, pp, own, got, w2, wh2, fs, fn, rhs)
        u = [x[i] + SCALE_Q * v3[f, i] for i in range(3)]
        y = fwd_second([below] + u + [above], w3, rhs)
        for i in range(3):
            x2[f, i] = x[i]
            x3[f, i] = y[i]
            eg[f, i] = edge(x0[f, i], half)
            eg[f, 3 + i] = edge(x1[f, i], half)
            eg[f, 6 + i] = edge(x[i], half)
            eg[f, 9 + i] = edge(y[i], half)

    fields(mid.shape[0], one)


def fixed(x, e):
    return jnp.concatenate([e[:PAD], x[PAD:-PAD], e[PAD:]], axis=0)


def turn_body(carry, fl, sc, x3, x2, eg, d3, d2, w3, w2, ra, *outs):
    if carry:
        outs[5][...] = outs[0][...]
        outs = outs[1:5]
    mid, pp, ss, sn = outs[:4]
    q = None if carry else outs[4]
    out = Sides(fl[2], ss, sn)
    rhs = ra[...]
    if q is not None:
        q[...] = jnp.zeros_like(q)
    scale = sc[0]

    def one(f):
        rows = []
        for i in range(3):
            y = fixed(x3[f, i], eg[f, 9 + i])
            t = d3[f, i] * y
            if q is not None:
                q[...] += fold(t * y)
            rows.append(t * scale)
        ends = [d2[f, i] * fixed(x2[f, i], eg[f, 6 + i]) * scale for i in (0, 2)]
        adj_pre(f, rows, w3, ends, w2, rhs, mid, pp, out)

    fields(x3.shape[0], one)


def rest_body(sc, x0, x1, x2, eg, d0, d1, d2, f0, f1, f2, q=None):
    if q is not None:
        q[...] = jnp.zeros_like(q)
    scale = sc[0]

    def one(f):
        for x, at, d, f_o in ((x0, 0, d0, f0), (x1, 3, d1, f1), (x2, 6, d2, f2)):
            for i in range(3):
                y = fixed(x[f, i], eg[f, at + i])
                t = d[f, i] * y
                if q is not None:
                    q[...] += fold(t * y)
                f_o[f, i] = t * scale

    fields(x0.shape[0], one)


def norm_body(v0, v1, v2, v3, q):
    q[...] = jnp.zeros_like(q)

    def one(f):
        for v in (v0, v1, v2, v3):
            for i in range(3):
                x = v[f, i]
                q[...] += fold(x * x)

    fields(v0.shape[0], one)


def lanes(shape):
    return lax.broadcasted_iota(jnp.int32, shape, len(shape) - 1)


def sums_body(n, *refs):
    out = refs[-1]
    parts = [refs[:n], refs[n : 3 * n], refs[3 * n : 4 * n]]
    acc = jnp.zeros(refs[0].shape, F32)
    at = 4 * n
    for _ in range(n):
        xs, ds = refs[at : at + 4], refs[at + 4 : at + 8]
        at += 8

        def one(f, acc):
            for x, d in zip(xs, ds):
                for i in range(3):
                    v = x[f, i]
                    acc = acc + fold(d[f, i] * v * v)
            return acc

        nf = xs[0].shape[0]
        acc = one(0, acc) if nf == 1 else lax.fori_loop(0, nf, one, acc)
    lane = lanes(out.shape)
    row = jnp.where(lane == 3, jnp.sum(acc, keepdims=True), 0.0)
    for k in range(3):
        val = parts[k][0][...]
        for p in parts[k][1:]:
            val = val + p[...]
        row = jnp.where(lane == k, jnp.sum(val, keepdims=True), row)
    out[...] = row


def add_body(a, b, out):
    out[...] = a[...] + b[...]


def ring_body(step, pos_ref, a, b, c, d, out):
    mine = lax.rem(lax.div(pos_ref[0], step), 4)
    rows = [a[...], b[...], c[...], d[...]]
    total = jnp.zeros(out.shape, F32)
    for place in range(4):
        gap = lax.rem(mine + 4 - place, 4)
        term = rows[0]
        for k in (1, 2, 3):
            term = jnp.where(gap == k, rows[k], term)
        total = total + term
    out[...] = total


def solve_body(hs, got, out):
    row = got[...]
    at = lanes(row.shape)

    def pick(k):
        return jnp.sum(jnp.where(at == k, row, 0.0), axis=1, keepdims=True)

    rr, bg, zz, bz = [pick(k) for k in range(4)]
    sig, inv = hs[0], hs[1]
    a0 = rr / (rr + bg)
    left = bg / (rr + bg)
    c = a0 * inv
    sbg = bg * sig
    rr1 = c * (c * (zz - sbg * (sbg / rr)))
    beta = rr1 / rr
    p = left + beta
    curve = p * (p * bg) - 2.0 * (p * (c * (inv * zz))) + c * (c * bz)
    a1 = rr1 / (rr1 + beta * beta * rr + curve)
    terms = (
        a0 + a1 * p,
        -(a1 * c),
        left - a1 * p,
        a1 * c - c - a1 * (p * inv),
        a1 * c,
    )
    w = jnp.zeros(row.shape, F32)
    for k, t in enumerate(terms):
        w = jnp.where(at == k, t, w)
    out[...] = w


def outbound_body(c_ref, v0, v1, v2, v3, out):
    v = (v0, v1, v2, v3)

    def put(first):
        for k in (first, first + 1):
            for f in range(out.shape[1]):
                for i in range(3):
                    out[k % 2, f, i] = v[k][f, i][PAD:-PAD]

    @pl.when(c_ref[0] == 0)
    def _():
        put(2)

    @pl.when(c_ref[0] != 0)
    def _():
        put(0)


def final_body(half, c_ref, k_ref, *refs):
    g, z, w = refs[0:4], refs[4:8], refs[8:12]
    og, oz, ow = refs[12:15]
    inc, res, ib, rb, sem = refs[15:]
    row = k_ref[...]
    at = lanes(row.shape)
    ig, iz, rg, rz, rw = [
        jnp.sum(jnp.where(at == k, row, 0.0), axis=1, keepdims=True) for k in range(5)
    ]
    c = c_ref[0]
    nf = og.shape[1]

    def put(first, mine, theirs):
        copies = []
        for k in (first, first + 1):
            n = k % 2
            for f in range(nf):
                for i in range(3):
                    x = [v[k][f, i][PAD:-PAD] for v in (g, z, w)]
                    y = [v[n, f, i] for v in (og, oz, ow)]
                    for (a, b, d), lo in ((x, mine), (y, theirs)):
                        ib[n, f, i, lo : lo + half] = ig * a + iz * b
                        rb[n, f, i, lo : lo + half] = rg * a + rz * b + rw * d
                for src, dst in ((ib, inc), (rb, res)):
                    copy = pltpu.make_async_copy(
                        src.at[n, f], dst.at[n, 0, f], sem.at[len(copies)]
                    )
                    copy.start()
                    copies.append(copy)
        for copy in copies:
            copy.wait()

    @pl.when(c == 0)
    def _():
        put(0, 0, half)

    @pl.when(c != 0)
    def _():
        put(2, half, 0)


def per_device(winds, mixing, innovations, obs_weight, obs_sub, obs_col, obs_count):
    owners, slots = obs_sub.shape[2], obs_sub.shape[3]
    lev = mixing.shape[0]
    cols = winds.shape[4]
    half = cols // 2
    wide = half + 2 * PAD
    cells = winds.shape[3] * cols
    c = lax.axis_index("tm").astype(jnp.int32)
    pos = lax.axis_index("space")
    bands = lax.axis_size("space")
    c_arr = c.reshape(1)
    pos_arr = pos.astype(jnp.int32).reshape(1)
    even = pos % 2 == 0
    flags = jnp.stack([pos > 0, pos < bands - 1, even]).astype(F32)
    first_pairs = [(i, i ^ 1) for i in range(bands)]
    second_pairs = [(i, (((i + 1) ^ 1) - 1) % bands) for i in range(bands)]

    def swap(x):
        return lax.ppermute(x, "tm", [(0, 1), (1, 0)])

    def exchange(a, b):
        return lax.ppermute(a, "space", first_pairs), lax.ppermute(b, "space", second_pairs)

    def ring_sum(row, step):
        shifts = []
        for k in (1, 2, 3):
            pairs = []
            for i in range(bands):
                digit = (i // step) % 4
                pairs.append((i, i + ((digit + k) % 4 - digit) * step))
            shifts.append(pairs)
        got = tuple(lax.ppermute(row, "space", p) for p in shifts)
        return call(
            functools.partial(ring_body, step),
            (pos_arr, row) + got,
            [SM] + [VM] * 4,
            [sds(1, lev)],
            flops=1e5,
        )[0]

    live = (
        jnp.arange(slots, dtype=jnp.int32)[None, :] < obs_count.reshape(owners)[:, None]
    )
    place = (obs_sub * cells + obs_col).reshape(owners, slots)
    place = jnp.where(live, place, -1).astype(F32)
    place = jnp.broadcast_to(place[..., None], (owners, slots, lev))
    blocks = 2 * FIELDS + 1
    packed, token = call(
        pack_body,
        (
            obs_weight.reshape(owners, slots, -1),
            innovations.reshape(owners, slots, -1),
            place,
        ),
        [VM] * 3,
        [sds(owners, blocks, slots, lev), sds(8, lev)],
    )
    got = lax.all_to_all(packed, "space", split_axis=0, concat_axis=0, tiled=True)

    w_own, w_snd, ra, rf = call(
        functools.partial(wind_body, half),
        (c_arr, winds[:, 0], mixing, token),
        [SM] + [VM] * 3,
        [sds(2, 2, 3, wide, lev)] * 2 + [sds(2 * lev, 2 * lev, dtype=BF16)] * 2,
    )
    w_got = swap(w_snd)
    w0, w1, w2, w3, down, up = call(
        pick_wind_body,
        (c_arr, w_own, w_got),
        [SM, VM, VM],
        [sds(2, 3, wide, lev)] * 4 + [sds(2, wide, lev)] * 2,
    )
    one_side, other_side = exchange(jnp.where(even, up, down), jnp.where(even, down, up))
    from_s = jnp.where(pos > 0, jnp.where(even, other_side, one_side), 0.0)
    from_n = jnp.where(pos < bands - 1, jnp.where(even, one_side, other_side), 0.0)
    wh0 = jnp.stack([from_s[0], from_n[0]])
    wh2 = jnp.stack([from_s[1], from_n[1]])

    size = jnp.abs(mixing)
    grow = (1.0 + MIXC * jnp.max(jnp.sum(size, 0))) * (1.0 + MIXC * jnp.max(jnp.sum(size, 1)))
    grow = grow * grow
    inv = grow * grow
    sig = 1.0 / inv
    sig_arr = sig.reshape(1)
    one_arr = jnp.ones((1,), F32)
    span = jnp.stack([sig, 1.0 / sig])

    flat = got.reshape(owners * blocks * slots, lev)
    flat, wh0, wh2, w0, w1, w2, w3, sig_arr, span = lax.optimization_barrier(
        (flat, wh0, wh2, w0, w1, w2, w3, sig_arr, span)
    )
    halves = [sds(2, FIELDS, 3, wide, lev)] * 2
    acc, g_own, g_snd = call(
        functools.partial(scatter_body, half, slots),
        (c_arr, flat),
        [SM, VM],
        [sds(2 * cells * 8, lev)] + halves,
        scratch=[
            pltpu.VMEM((slots, lev), jnp.int32),
            pltpu.SMEM((slots, lev), jnp.int32),
            pltpu.SemaphoreType.DMA(()),
        ],
    )
    g_got = swap(g_snd)
    d_own, d_snd = call(functools.partial(diag_body, half), (c_arr, acc), [SM, VM], halves)
    d_got = swap(d_snd)
    groups = []
    f0 = 0
    for nf in GROUPS:
        shapes = [sds(nf, 3, wide, lev)] * 4
        pick = functools.partial(pick_body, f0)
        gg = call(pick, (c_arr, g_own, g_got), [SM, VM, VM], shapes)
        dd = call(pick, (c_arr, d_own, d_got), [SM, VM, VM], shapes)
        groups.append((nf, gg, dd))
        f0 += nf

    part = sds(8, lev)

    def row3(nf):
        return sds(nf, 3, wide, lev)

    def state_of(nf, n):
        return [sds(nf, wide, lev)] + [sds(n, nf, wide, lev)] * 3

    def adj_mid(state, f2, f1, f0, row=None):
        mid, pp, ss, sn = state
        nf = mid.shape[0]
        rs, rn = exchange(ss, sn)
        carry = row is not None
        ins = (flags, mid, pp, ss, sn, rs, rn, f2, f1, f0, w2, wh2, w1, w0, ra)
        ins += (row,) if carry else ()
        o = call(
            functools.partial(adj_mid_body, carry),
            ins,
            [SM] + [VM] * (len(ins) - 1),
            [row3(nf)] * 2 + state_of(nf, 2) + ([sds(1, lev)] if carry else []),
        )
        if carry:
            return o[0], o[1], tuple(o[2:6]), o[6]
        return o[0], o[1], tuple(o[2:])

    def adj_last(state, f0, more):
        mid, pp, ss, sn = state
        nf = mid.shape[0]
        rs, rn = exchange(ss, sn)
        ins = (flags, mid, pp, ss, sn, rs, rn, f0, w0, wh0, ra, rf)
        outs = [row3(nf)] * 2 + (state_of(nf, 2) if more else [])
        o = call(
            functools.partial(adj_last_body, more), ins, [SM] + [VM] * (len(ins) - 1), outs
        )
        return o[0], o[1], tuple(o[2:])

    def forward(state, v):
        mid, pp, ss, sn = state
        nf = mid.shape[0]
        rs, rn = exchange(ss, sn)
        ins = (flags, mid, pp, ss, sn, rs, rn, v[1], v[2], v[3], w0, wh0, w1, w2, rf)
        o = call(
            fwd_first_body,
            ins,
            [SM] + [VM] * (len(ins) - 1),
            [row3(nf)] * 2 + state_of(nf, 2),
        )
        x0, x1, mid, pp, ss, sn = o
        rs, rn = exchange(ss, sn)
        ins = (flags, mid, pp, ss, sn, rs, rn, v[3], x0, x1, w2, wh2, w3, rf)
        o = call(
            functools.partial(fwd_last_body, half),
            ins,
            [SM] + [VM] * (len(ins) - 1),
            [row3(nf)] * 2 + [sds(nf, 12, 2 * PAD, lev)],
        )
        return (x0, x1, o[0], o[1]), o[2]

    def turn(xs, eg, dd, scale, row=None):
        eg = swap(eg)
        x0, x1, x2, x3 = xs
        nf = x3.shape[0]
        carry = row is not None
        ins = (flags, scale, x3, x2, eg, dd[3], dd[2], w3, w2, ra)
        ins += (row,) if carry else ()
        o = call(
            functools.partial(turn_body, carry),
            ins,
            [SM] * 2 + [VM] * (len(ins) - 2),
            state_of(nf, 2) + [sds(1, lev) if carry else part],
        )
        r = call(
            rest_body,
            (scale, x0, x1, x2, eg, dd[0], dd[1], dd[2]),
            [SM] + [VM] * 7,
            [row3(nf)] * 3 + ([] if carry else [part]),
        )
        return tuple(o[:4]), tuple(r[:3]), (o[4] if carry else (o[4], r[3]))

    def norm(v):
        return call(norm_body, tuple(v), [VM] * 4, [part])[0]

    chains = []
    for nf, gg, dd in groups:
        state = tuple(
            call(
                turn_first_body,
                (flags, gg[3], gg[2], w3, w2, ra),
                [SM] + [VM] * 5,
                state_of(nf, 2),
            )
        )
        g3, g2, state = adj_mid(state, gg[2], gg[1], gg[0])
        g0, g1, state = adj_last(state, gg[0], True)
        g = (g0, g1, g2, g3)
        xs, eg = forward(state, g)
        state, fs, bg = turn(xs, eg, dd, sig_arr)
        z3, z2, state = adj_mid(state, fs[2], fs[1], fs[0])
        z0, z1, state = adj_last(state, fs[0], True)
        z = (z0, z1, z2, z3)
        xs, eg = forward(state, z)
        chains.append((g, z, xs, eg, norm(g), bg, norm(z)))
    ins = [ch[4] for ch in chains] + [q for ch in chains for q in ch[5]]
    ins += [ch[6] for ch in chains]
    for ch, (_, _, dd) in zip(chains, groups):
        ins += list(ch[2]) + list(dd)
    row = call(
        functools.partial(sums_body, len(chains)), tuple(ins), [VM] * len(ins), [sds(1, lev)]
    )[0]
    row = call(add_body, (row, swap(row)), [VM] * 2, [sds(1, lev)], flops=1e5)[0]
    states = []
    for ch, (nf, gg, dd) in zip(chains, groups):
        state, fs, row = turn(ch[2], ch[3], dd, one_arr, row)
        states.append((state, fs))
    row = ring_sum(ring_sum(row, 1), 4)
    mids = []
    for state, fs in states:
        w3z, w2z, state, row = adj_mid(state, fs[2], fs[1], fs[0], row)
        mids.append((w3z, w2z, state, fs))
    row = ring_sum(row, 16)
    weights = call(solve_body, (span, row), [SM, VM], [sds(1, lev)], flops=1e5)[0]

    g, z = chains[0][0], chains[0][1]
    w3z, w2z, state, fs = mids[0]
    w0z, w1z, _ = adj_last(state, fs[0], False)
    w = (w0z, w1z, w2z, w3z)
    shape = sds(2, FIELDS, 3, half, lev)

    def other(v):
        return swap(
            call(outbound_body, (c_arr,) + tuple(v), [SM] + [VM] * 4, [shape])[0]
        )

    ins = (c_arr, weights) + tuple(g) + tuple(z) + w + (other(g), other(z), other(w))
    full = (2, FIELDS, 3, cols, lev)
    return call(
        functools.partial(final_body, half),
        ins,
        [SM] + [VM] * (len(ins) - 1),
        [sds(2, 1, FIELDS, 3, cols, lev)] * 2,
        scratch=[
            pltpu.VMEM(full, F32),
            pltpu.VMEM(full, F32),
            pltpu.SemaphoreType.DMA((4 * FIELDS,)),
        ],
        out_specs=[pl.BlockSpec(memory_space=pl.ANY)] * 2,
        vmem=12 * 2**20,
    )


def solution(mesh):
    in_specs = (
        P("tm", "space", None, None, None, None),
        P(),
        P("tm", "space", None, None, None),
        P("tm", "space", None, None, None),
        P("tm", "space", None, None),
        P("tm", "space", None, None),
        P("tm", "space", None),
    )
    out_specs = (P("tm", "space", None, None, None, None), P("tm", "space", None, None, None, None))
    return jax.shard_map(
        per_device, mesh=mesh, in_specs=in_specs, out_specs=out_specs, check_vma=False
    )
```

```python
import functools
import jax
import jax.numpy as jnp
from jax import lax
from jax.experimental import pallas as pl
from jax.experimental.pallas import tpu as pltpu
from jax.sharding import PartitionSpec as P

FIELDS = 3
MIXC = 0.25
SCALE_Q = 0.5
GROUPS = (FIELDS,)
PAD = 8
F32 = jnp.float32
BF16 = jnp.bfloat16

VM = pl.BlockSpec(memory_space=pltpu.VMEM)
SM = pl.BlockSpec(memory_space=pltpu.SMEM)


def call(body, ins, specs, outs, vmem=None, flops=1e8, scratch=(), out_specs=None):
    nbytes = sum(a.size * a.dtype.itemsize for a in ins)
    nbytes += sum(o.size * o.dtype.itemsize for o in outs)
    return pl.pallas_call(
        body,
        out_shape=outs,
        in_specs=specs,
        out_specs=out_specs or [VM] * len(outs),
        scratch_shapes=list(scratch),
        compiler_params=pltpu.CompilerParams(vmem_limit_bytes=vmem or 6 * 2**20),
        cost_estimate=pl.CostEstimate(
            flops=int(flops), bytes_accessed=int(nbytes), transcendentals=0
        ),
    )(*ins)


def sds(*shape, dtype=F32):
    return jax.ShapeDtypeStruct(shape, dtype)


def later(x):
    return pltpu.roll(x, 1, 0)


def earlier(x):
    return pltpu.roll(x, x.shape[0] - 1, 0)


def coef(w_ref, i):
    a = w_ref[0, i]
    b = w_ref[1, i]
    ap = jnp.maximum(a, 0.0)
    am = ap - a
    bp = jnp.maximum(b, 0.0)
    bm = bp - b
    return ap, am, bp, bm, 1.0 - (ap + am) - (bp + bm)


def mixed(v, rhs):
    lev = v.shape[1]
    hi = v.astype(BF16)
    lo = (v - hi.astype(F32)).astype(BF16)
    o = jnp.dot(jnp.concatenate([hi, lo], axis=1), rhs, preferred_element_type=F32)
    return v + (o[:, :lev] + o[:, lev:])


class Sides:

    def __init__(self, flag, first, second):
        self.even = flag > 0.5
        self.refs = (first, second)

    def south(self, k, f):
        return jnp.where(self.even, self.refs[1][k, f], self.refs[0][k, f])

    def north(self, k, f):
        return jnp.where(self.even, self.refs[0][k, f], self.refs[1][k, f])

    def put(self, k, f, south, north):
        self.refs[0][k, f] = jnp.where(self.even, north, south)
        self.refs[1][k, f] = jnp.where(self.even, south, north)


def adj_local(w, c):
    ap, am, _, _, c0 = c
    return c0 * w + earlier(ap * w) + later(am * w)


def fwd_local(u, c):
    ap, am, _, _, c0 = c
    return c0 * u + ap * later(u) + am * earlier(u)


def adj_pre(f, rows, w_ref, ends, next_ref, rhs, mid_ref, pp_ref, out):
    w = [mixed(x, rhs) for x in rows]
    c = [coef(w_ref, i) for i in range(3)]
    low = adj_local(w[0], c[0]) + c[1][2] * w[1]
    high = adj_local(w[2], c[2]) + c[1][3] * w[1]
    mid_ref[f] = adj_local(w[1], c[1]) + c[2][2] * w[2] + c[0][3] * w[0]
    pp_ref[0, f] = low
    pp_ref[1, f] = high
    south = jnp.maximum(next_ref[1, 0], 0.0) * mixed(low + ends[0], rhs)
    north = jnp.maximum(-next_ref[1, 2], 0.0) * mixed(high + ends[1], rhs)
    out.put(0, f, south, north)
    out.put(1, f, c[0][2] * w[0], c[2][3] * w[2])


def adj_post(f, mid_ref, pp_ref, got, fs, fn):
    return [
        pp_ref[0, f] + got.south(1, f) * fs,
        mid_ref[f],
        pp_ref[1, f] + got.north(1, f) * fn,
    ]


def adj_second(f, rows, w_ref, wh_ref, rhs, own, got, fs, fn):
    w = [mixed(x, rhs) for x in rows]
    c = [coef(w_ref, i) for i in range(3)]
    below = got.south(0, f) * fs + wh_ref[0] * mixed(own.south(1, f), rhs)
    above = got.north(0, f) * fn + wh_ref[1] * mixed(own.north(1, f), rhs)
    return [
        adj_local(w[0], c[0]) + c[1][2] * w[1] + below,
        adj_local(w[1], c[1]) + c[2][2] * w[2] + c[0][3] * w[0],
        adj_local(w[2], c[2]) + c[1][3] * w[1] + above,
    ]


def fwd_pre(f, u, w_ref, ends, rhs, mid_ref, pp_ref, out):
    c = [coef(w_ref, i) for i in range(3)]
    low = fwd_local(u[0], c[0]) + c[0][3] * u[1]
    high = fwd_local(u[2], c[2]) + c[2][2] * u[1]
    mid_ref[f] = fwd_local(u[1], c[1]) + c[1][2] * u[0] + c[1][3] * u[2]
    pp_ref[0, f] = low
    pp_ref[1, f] = high
    out.put(0, f, u[0], u[2])
    out.put(1, f, mixed(low, rhs) + ends[0], mixed(high, rhs) + ends[1])


def fwd_post(f, mid_ref, pp_ref, own, got, w_ref, wh_ref, fs, fn, rhs):
    b0 = w_ref[1, 0]
    b2 = w_ref[1, 2]
    m = [
        pp_ref[0, f] + jnp.maximum(b0, 0.0) * (got.south(0, f) * fs),
        mid_ref[f],
        pp_ref[1, f] + jnp.maximum(-b2, 0.0) * (got.north(0, f) * fn),
    ]
    below = (got.south(1, f) + mixed(wh_ref[0] * own.south(0, f), rhs)) * fs
    above = (got.north(1, f) + mixed(wh_ref[1] * own.north(0, f), rhs)) * fn
    return [mixed(x, rhs) for x in m], below, above


def fwd_second(u5, w_ref, rhs):
    out = []
    for i in range(3):
        c = coef(w_ref, i)
        m = fwd_local(u5[i + 1], c) + c[2] * u5[i] + c[3] * u5[i + 2]
        out.append(mixed(m, rhs))
    return out


def fields(n, body):
    if n == 1:
        body(0)
        return

    def step(f, carry):
        body(f)
        return carry

    lax.fori_loop(0, n, step, 0)


def fold(x):
    own = x[PAD:-PAD]
    return jnp.sum(own.reshape(own.shape[0] // 8, 8, own.shape[1]), axis=0)


def split_store(x, half, c, own_ref, snd_ref, idx):
    n = x.shape[0]
    low = jnp.concatenate([x[n - PAD :], x[: half + PAD]], axis=0)
    high = jnp.concatenate([x[half - PAD :], x[:PAD]], axis=0)

    @pl.when(c == 0)
    def _():
        own_ref[idx] = low
        snd_ref[idx] = high

    @pl.when(c != 0)
    def _():
        own_ref[idx] = high
        snd_ref[idx] = low


def pack_body(w_ref, d_ref, i_ref, o_ref, t_ref):
    t_ref[...] = jnp.zeros_like(t_ref)
    lev = o_ref.shape[-1]
    live = i_ref[...] >= 0.0
    for f in range(FIELDS):
        w = jnp.where(live, w_ref[:, :, f * lev : (f + 1) * lev], 0.0)
        o_ref[:, f] = w
        o_ref[:, FIELDS + f] = w * d_ref[:, :, f * lev : (f + 1) * lev]
    o_ref[:, 2 * FIELDS] = i_ref[...]


def emit(half, c, acc, at, own_ref, snd_ref):
    cols = 2 * half
    for w in range(2):

        def one(i, carry):
            base = (w * 3 + i) * (cols * 8) + at
            for f in range(FIELDS):
                x = acc[pl.ds(base + f, cols, stride=8), :]
                split_store(x, half, c, own_ref, snd_ref, (w, f, i))
            return carry

        lax.fori_loop(0, 3, one, 0)


def scatter_body(half, slots, c_ref, p_ref, acc, go_ref, gs_ref, idx_v, idx_s, sem):
    blocks = 2 * FIELDS + 1
    owners = p_ref.shape[0] // (blocks * slots)
    lev = p_ref.shape[1]
    lane = lanes((slots, lev))

    def column(o, vals):
        at = pl.multiple_of((o * blocks + blocks - 1) * slots, slots)
        return jnp.where(lane == o, p_ref[pl.ds(at, slots), :], vals)

    vals = lax.fori_loop(0, owners, column, jnp.zeros((slots, lev), F32))
    idx_v[...] = jnp.maximum(vals, 0.0).astype(jnp.int32)
    copy = pltpu.make_async_copy(idx_v, idx_s, sem)
    copy.start()
    cells = acc.shape[0] // 8
    chunk = 64

    def clear(t, carry):
        acc[pl.ds(pl.multiple_of(t * (8 * chunk), 8 * chunk), 8 * chunk), :] = jnp.zeros(
            (8 * chunk, lev), F32
        )
        return carry

    lax.fori_loop(0, cells // chunk, clear, 0)

    copy.wait()

    def put(o, carry):
        for s in range(slots):
            row = pl.multiple_of(idx_s[s, o] * 8, 8)
            x = p_ref[pl.ds(o * (blocks * slots) + s, blocks, stride=slots), :]
            acc[pl.ds(row, blocks), :] += x
        return carry

    lax.fori_loop(0, owners, put, 0)
    emit(half, c_ref[0], acc, FIELDS, go_ref, gs_ref)


def diag_body(half, c_ref, acc, do_ref, ds_ref):
    emit(half, c_ref[0], acc, 0, do_ref, ds_ref)


def wind_body(half, c_ref, w_ref, m_ref, t_ref, o_ref, s_ref, ra_ref, rf_ref):
    c = c_ref[0]
    for w in range(2):

        def one(i, carry):
            for k in range(2):
                split_store(w_ref[w, k, i].astype(F32), half, c, o_ref, s_ref, (w, k, i))
            return carry

        lax.fori_loop(0, 3, one, 0)
    for m, ref in ((m_ref[...] * MIXC, ra_ref), (m_ref[...].T * MIXC, rf_ref)):
        hi = m.astype(BF16)
        lo = (m - hi.astype(F32)).astype(BF16)
        line = jnp.concatenate([hi, lo], axis=1)
        ref[...] = jnp.concatenate([line, line], axis=0)


def pick_body(f0, c_ref, own_ref, got_ref, *outs):
    c = c_ref[0]
    nf = outs[0].shape[0]

    def put(src, dst):
        for w in range(2):
            for f in range(nf):
                dst[w][f] = src[w, f0 + f]

    @pl.when(c == 0)
    def _():
        put(own_ref, outs[:2])
        put(got_ref, outs[2:4])

    @pl.when(c != 0)
    def _():
        put(got_ref, outs[:2])
        put(own_ref, outs[2:4])


def pick_wind_body(c_ref, own_ref, got_ref, w0, w1, w2, w3, ss, sn):
    pick_body(0, c_ref, own_ref, got_ref, w0, w1, w2, w3)
    for k, w in enumerate((w0, w2)):
        ss[k] = jnp.maximum(w[1, 0], 0.0)
        sn[k] = jnp.maximum(-w[1, 2], 0.0)


def turn_first_body(fl, g3, g2, w3, w2, ra, mid, pp, ss, sn):
    rhs = ra[...]
    out = Sides(fl[2], ss, sn)

    def one(f):
        rows = [g3[f, i] for i in range(3)]
        adj_pre(f, rows, w3, (g2[f, 0], g2[f, 2]), w2, rhs, mid, pp, out)

    fields(g3.shape[0], one)


def adj_mid_body(carry, *refs):
    if carry:
        refs[-1][...] = refs[15][...]
        refs = refs[:15] + refs[16:-1]
    (fl, mid, pp, ss, sn, rs, rn, f2, f1, f0, w2, wh2, w1, w0, ra) = refs[:15]
    g3, g2, mid_o, pp_o, ss_o, sn_o = refs[15:]
    fs, fn = fl[0], fl[1]
    rhs = ra[...]
    own, got, out_o = Sides(fl[2], ss, sn), Sides(fl[2], rs, rn), Sides(fl[2], ss_o, sn_o)

    def one(f):
        lam = adj_post(f, mid, pp, got, fs, fn)
        for i in range(3):
            g3[f, i] = lam[i] * SCALE_Q
        rows = [lam[i] + f2[f, i] for i in range(3)]
        out = adj_second(f, rows, w2, wh2, rhs, own, got, fs, fn)
        for i in range(3):
            g2[f, i] = out[i] * SCALE_Q
        rows = [out[i] + f1[f, i] for i in range(3)]
        adj_pre(f, rows, w1, (f0[f, 0], f0[f, 2]), w0, rhs, mid_o, pp_o, out_o)

    fields(mid.shape[0], one)


def adj_last_body(more, *refs):
    (fl, mid, pp, ss, sn, rs, rn, f0, w0, wh0, ra, rf) = refs[:12]
    outs = refs[12:]
    fs, fn = fl[0], fl[1]
    rhs = ra[...]
    own, got = Sides(fl[2], ss, sn), Sides(fl[2], rs, rn)
    if more:
        out_o = Sides(fl[2], outs[4], outs[5])

    def one(f):
        lam = adj_post(f, mid, pp, got, fs, fn)
        rows = [lam[i] + f0[f, i] for i in range(3)]
        out = adj_second(f, rows, w0, wh0, rhs, own, got, fs, fn)
        for i in range(3):
            outs[1][f, i] = lam[i] * SCALE_Q
            outs[0][f, i] = out[i]
        if more:
            half = SCALE_Q * SCALE_Q
            ends = (half * lam[0], half * lam[2])
            fwd_pre(f, out, w0, ends, rf[...], outs[2], outs[3], out_o)

    fields(mid.shape[0], one)


def fwd_first_body(fl, mid, pp, ss, sn, rs, rn, v1, v2, v3, w0, wh0, w1, w2, rf, *outs):
    x0, x1, mid_o, pp_o, ss_o, sn_o = outs
    fs, fn = fl[0], fl[1]
    rhs = rf[...]
    own, got, out_o = Sides(fl[2], ss, sn), Sides(fl[2], rs, rn), Sides(fl[2], ss_o, sn_o)

    def one(f):
        x, below, above = fwd_post(f, mid, pp, own, got, w0, wh0, fs, fn, rhs)
        for i in range(3):
            x0[f, i] = x[i]
        u = [x[i] + SCALE_Q * v1[f, i] for i in range(3)]
        x = fwd_second([below] + u + [above], w1, rhs)
        for i in range(3):
            x1[f, i] = x[i]
        u = [x[i] + SCALE_Q * v2[f, i] for i in range(3)]
        ends = (SCALE_Q * v3[f, 0], SCALE_Q * v3[f, 2])
        fwd_pre(f, u, w2, ends, rhs, mid_o, pp_o, out_o)

    fields(mid.shape[0], one)


def edge(x, half):
    return jnp.concatenate([x[half : half + PAD], x[PAD : 2 * PAD]], axis=0)


def fwd_last_body(half, fl, mid, pp, ss, sn, rs, rn, v3, x0, x1, w2, wh2, w3, rf, *outs):
    x2, x3, eg = outs
    fs, fn = fl[0], fl[1]
    rhs = rf[...]
    own, got = Sides(fl[2], ss, sn), Sides(fl[2], rs, rn)

    def one(f):
        x, below, above = fwd_post(f, mid, pp, own, got, w2, wh2, fs, fn, rhs)
        u = [x[i] + SCALE_Q * v3[f, i] for i in range(3)]
        y = fwd_second([below] + u + [above], w3, rhs)
        for i in range(3):
            x2[f, i] = x[i]
            x3[f, i] = y[i]
            eg[f, i] = edge(x0[f, i], half)
            eg[f, 3 + i] = edge(x1[f, i], half)
            eg[f, 6 + i] = edge(x[i], half)
            eg[f, 9 + i] = edge(y[i], half)

    fields(mid.shape[0], one)


def fixed(x, e):
    return jnp.concatenate([e[:PAD], x[PAD:-PAD], e[PAD:]], axis=0)


def turn_body(carry, fl, sc, x3, x2, eg, d3, d2, w3, w2, ra, *outs):
    if carry:
        outs[5][...] = outs[0][...]
        outs = outs[1:5]
    mid, pp, ss, sn = outs[:4]
    q = None if carry else outs[4]
    out = Sides(fl[2], ss, sn)
    rhs = ra[...]
    if q is not None:
        q[...] = jnp.zeros_like(q)
    scale = sc[0]

    def one(f):
        rows = []
        for i in range(3):
            y = fixed(x3[f, i], eg[f, 9 + i])
            t = d3[f, i] * y
            if q is not None:
                q[...] += fold(t * y)
            rows.append(t * scale)
        ends = [d2[f, i] * fixed(x2[f, i], eg[f, 6 + i]) * scale for i in (0, 2)]
        adj_pre(f, rows, w3, ends, w2, rhs, mid, pp, out)

    fields(x3.shape[0], one)


def rest_body(sc, x0, x1, x2, eg, d0, d1, d2, f0, f1, f2, q=None):
    if q is not None:
        q[...] = jnp.zeros_like(q)
    scale = sc[0]

    def one(f):
        for x, at, d, f_o in ((x0, 0, d0, f0), (x1, 3, d1, f1), (x2, 6, d2, f2)):
            for i in range(3):
                y = fixed(x[f, i], eg[f, at + i])
                t = d[f, i] * y
                if q is not None:
                    q[...] += fold(t * y)
                f_o[f, i] = t * scale

    fields(x0.shape[0], one)


def norm_body(v0, v1, v2, v3, q):
    q[...] = jnp.zeros_like(q)

    def one(f):
        for v in (v0, v1, v2, v3):
            for i in range(3):
                x = v[f, i]
                q[...] += fold(x * x)

    fields(v0.shape[0], one)


def lanes(shape):
    return lax.broadcasted_iota(jnp.int32, shape, len(shape) - 1)


def sums_body(n, *refs):
    out = refs[-1]
    parts = [refs[:n], refs[n : 3 * n], refs[3 * n : 4 * n]]
    acc = jnp.zeros(refs[0].shape, F32)
    at = 4 * n
    for _ in range(n):
        xs, ds = refs[at : at + 4], refs[at + 4 : at + 8]
        at += 8

        def one(f, acc):
            for x, d in zip(xs, ds):
                for i in range(3):
                    v = x[f, i]
                    acc = acc + fold(d[f, i] * v * v)
            return acc

        nf = xs[0].shape[0]
        acc = one(0, acc) if nf == 1 else lax.fori_loop(0, nf, one, acc)
    lane = lanes(out.shape)
    row = jnp.where(lane == 3, jnp.sum(acc, keepdims=True), 0.0)
    for k in range(3):
        val = parts[k][0][...]
        for p in parts[k][1:]:
            val = val + p[...]
        row = jnp.where(lane == k, jnp.sum(val, keepdims=True), row)
    out[...] = row


def add_body(a, b, out):
    out[...] = a[...] + b[...]


def ring_body(step, pos_ref, a, b, c, d, out):
    mine = lax.rem(lax.div(pos_ref[0], step), 4)
    rows = [a[...], b[...], c[...], d[...]]
    total = jnp.zeros(out.shape, F32)
    for place in range(4):
        gap = lax.rem(mine + 4 - place, 4)
        term = rows[0]
        for k in (1, 2, 3):
            term = jnp.where(gap == k, rows[k], term)
        total = total + term
    out[...] = total


def solve_body(hs, got, out):
    row = got[...]
    at = lanes(row.shape)

    def pick(k):
        return jnp.sum(jnp.where(at == k, row, 0.0), axis=1, keepdims=True)

    rr, bg, zz, bz = [pick(k) for k in range(4)]
    sig, inv = hs[0], hs[1]
    a0 = rr / (rr + bg)
    left = bg / (rr + bg)
    c = a0 * inv
    sbg = bg * sig
    rr1 = c * (c * (zz - sbg * (sbg / rr)))
    beta = rr1 / rr
    p = left + beta
    curve = p * (p * bg) - 2.0 * (p * (c * (inv * zz))) + c * (c * bz)
    a1 = rr1 / (rr1 + beta * beta * rr + curve)
    terms = (
        a0 + a1 * p,
        -(a1 * c),
        left - a1 * p,
        a1 * c - c - a1 * (p * inv),
        a1 * c,
    )
    w = jnp.zeros(row.shape, F32)
    for k, t in enumerate(terms):
        w = jnp.where(at == k, t, w)
    out[...] = w


def outbound_body(c_ref, v0, v1, v2, v3, out):
    v = (v0, v1, v2, v3)

    def put(first):
        for k in (first, first + 1):
            for f in range(out.shape[1]):
                for i in range(3):
                    out[k % 2, f, i] = v[k][f, i][PAD:-PAD]

    @pl.when(c_ref[0] == 0)
    def _():
        put(2)

    @pl.when(c_ref[0] != 0)
    def _():
        put(0)


def final_body(half, c_ref, k_ref, *refs):
    g, z, w = refs[0:4], refs[4:8], refs[8:12]
    og, oz, ow = refs[12:15]
    inc, res, ib, rb, sem = refs[15:]
    row = k_ref[...]
    at = lanes(row.shape)
    ig, iz, rg, rz, rw = [
        jnp.sum(jnp.where(at == k, row, 0.0), axis=1, keepdims=True) for k in range(5)
    ]
    c = c_ref[0]
    nf = og.shape[1]

    def put(first, mine, theirs):
        copies = []
        for k in (first, first + 1):
            n = k % 2
            for f in range(nf):
                for i in range(3):
                    x = [v[k][f, i][PAD:-PAD] for v in (g, z, w)]
                    y = [v[n, f, i] for v in (og, oz, ow)]
                    for (a, b, d), lo in ((x, mine), (y, theirs)):
                        ib[n, f, i, lo : lo + half] = ig * a + iz * b
                        rb[n, f, i, lo : lo + half] = rg * a + rz * b + rw * d
                for src, dst in ((ib, inc), (rb, res)):
                    copy = pltpu.make_async_copy(
                        src.at[n, f], dst.at[n, 0, f], sem.at[len(copies)]
                    )
                    copy.start()
                    copies.append(copy)
        for copy in copies:
            copy.wait()

    @pl.when(c == 0)
    def _():
        put(0, 0, half)

    @pl.when(c != 0)
    def _():
        put(2, half, 0)


def per_device(winds, mixing, innovations, obs_weight, obs_sub, obs_col, obs_count):
    owners, slots = obs_sub.shape[2], obs_sub.shape[3]
    lev = mixing.shape[0]
    cols = winds.shape[4]
    half = cols // 2
    wide = half + 2 * PAD
    cells = winds.shape[3] * cols
    c = lax.axis_index("tm").astype(jnp.int32)
    pos = lax.axis_index("space")
    bands = lax.axis_size("space")
    c_arr = c.reshape(1)
    pos_arr = pos.astype(jnp.int32).reshape(1)
    even = pos % 2 == 1
    flags = jnp.stack([pos > 0, pos < bands - 1, even]).astype(F32)
    first_pairs = [(i, (((i + 1) ^ 1) - 1) % bands) for i in range(bands)]
    second_pairs = [(i, i ^ 1) for i in range(bands)]

    def swap(x):
        return lax.ppermute(x, "tm", [(0, 1), (1, 0)])

    def exchange(a, b):
        return lax.ppermute(a, "space", first_pairs), lax.ppermute(b, "space", second_pairs)

    def ring_sum(row, step):
        shifts = []
        for k in (1, 2, 3):
            pairs = []
            for i in range(bands):
                digit = (i // step) % 4
                pairs.append((i, i + ((digit + k) % 4 - digit) * step))
            shifts.append(pairs)
        got = tuple(lax.ppermute(row, "space", p) for p in shifts)
        return call(
            functools.partial(ring_body, step),
            (pos_arr, row) + got,
            [SM] + [VM] * 4,
            [sds(1, lev)],
            flops=1e5,
        )[0]

    live = (
        jnp.arange(slots, dtype=jnp.int32)[None, :] < obs_count.reshape(owners)[:, None]
    )
    place = (obs_sub * cells + obs_col).reshape(owners, slots)
    place = jnp.where(live, place, -1).astype(F32)
    place = jnp.broadcast_to(place[..., None], (owners, slots, lev))
    blocks = 2 * FIELDS + 1
    packed, token = call(
        pack_body,
        (
            obs_weight.reshape(owners, slots, -1),
            innovations.reshape(owners, slots, -1),
            place,
        ),
        [VM] * 3,
        [sds(owners, blocks, slots, lev), sds(8, lev)],
    )
    got = lax.all_to_all(packed, "space", split_axis=0, concat_axis=0, tiled=True)

    w_own, w_snd, ra, rf = call(
        functools.partial(wind_body, half),
        (c_arr, winds[:, 0], mixing, token),
        [SM] + [VM] * 3,
        [sds(2, 2, 3, wide, lev)] * 2 + [sds(2 * lev, 2 * lev, dtype=BF16)] * 2,
    )
    w_got = swap(w_snd)
    w0, w1, w2, w3, down, up = call(
        pick_wind_body,
        (c_arr, w_own, w_got),
        [SM, VM, VM],
        [sds(2, 3, wide, lev)] * 4 + [sds(2, wide, lev)] * 2,
    )
    one_side, other_side = exchange(jnp.where(even, up, down), jnp.where(even, down, up))
    from_s = jnp.where(pos > 0, jnp.where(even, other_side, one_side), 0.0)
    from_n = jnp.where(pos < bands - 1, jnp.where(even, one_side, other_side), 0.0)
    wh0 = jnp.stack([from_s[0], from_n[0]])
    wh2 = jnp.stack([from_s[1], from_n[1]])

    size = jnp.abs(mixing)
    grow = (1.0 + MIXC * jnp.max(jnp.sum(size, 0))) * (1.0 + MIXC * jnp.max(jnp.sum(size, 1)))
    grow = grow * grow
    inv = grow * grow
    sig = 1.0 / inv
    sig_arr = sig.reshape(1)
    one_arr = jnp.ones((1,), F32)
    span = jnp.stack([sig, 1.0 / sig])

    flat = got.reshape(owners * blocks * slots, lev)
    flat, wh0, wh2, w0, w1, w2, w3, sig_arr, span = lax.optimization_barrier(
        (flat, wh0, wh2, w0, w1, w2, w3, sig_arr, span)
    )
    halves = [sds(2, FIELDS, 3, wide, lev)] * 2
    acc, g_own, g_snd = call(
        functools.partial(scatter_body, half, slots),
        (c_arr, flat),
        [SM, VM],
        [sds(2 * cells * 8, lev)] + halves,
        scratch=[
            pltpu.VMEM((slots, lev), jnp.int32),
            pltpu.SMEM((slots, lev), jnp.int32),
            pltpu.SemaphoreType.DMA(()),
        ],
    )
    g_got = swap(g_snd)
    d_own, d_snd = call(functools.partial(diag_body, half), (c_arr, acc), [SM, VM], halves)
    d_got = swap(d_snd)
    groups = []
    f0 = 0
    for nf in GROUPS:
        shapes = [sds(nf, 3, wide, lev)] * 4
        pick = functools.partial(pick_body, f0)
        gg = call(pick, (c_arr, g_own, g_got), [SM, VM, VM], shapes)
        dd = call(pick, (c_arr, d_own, d_got), [SM, VM, VM], shapes)
        groups.append((nf, gg, dd))
        f0 += nf

    part = sds(8, lev)

    def row3(nf):
        return sds(nf, 3, wide, lev)

    def state_of(nf, n):
        return [sds(nf, wide, lev)] + [sds(n, nf, wide, lev)] * 3

    def adj_mid(state, f2, f1, f0, row=None):
        mid, pp, ss, sn = state
        nf = mid.shape[0]
        rs, rn = exchange(ss, sn)
        carry = row is not None
        ins = (flags, mid, pp, ss, sn, rs, rn, f2, f1, f0, w2, wh2, w1, w0, ra)
        ins += (row,) if carry else ()
        o = call(
            functools.partial(adj_mid_body, carry),
            ins,
            [SM] + [VM] * (len(ins) - 1),
            [row3(nf)] * 2 + state_of(nf, 2) + ([sds(1, lev)] if carry else []),
        )
        if carry:
            return o[0], o[1], tuple(o[2:6]), o[6]
        return o[0], o[1], tuple(o[2:])

    def adj_last(state, f0, more):
        mid, pp, ss, sn = state
        nf = mid.shape[0]
        rs, rn = exchange(ss, sn)
        ins = (flags, mid, pp, ss, sn, rs, rn, f0, w0, wh0, ra, rf)
        outs = [row3(nf)] * 2 + (state_of(nf, 2) if more else [])
        o = call(
            functools.partial(adj_last_body, more), ins, [SM] + [VM] * (len(ins) - 1), outs
        )
        return o[0], o[1], tuple(o[2:])

    def forward(state, v):
        mid, pp, ss, sn = state
        nf = mid.shape[0]
        rs, rn = exchange(ss, sn)
        ins = (flags, mid, pp, ss, sn, rs, rn, v[1], v[2], v[3], w0, wh0, w1, w2, rf)
        o = call(
            fwd_first_body,
            ins,
            [SM] + [VM] * (len(ins) - 1),
            [row3(nf)] * 2 + state_of(nf, 2),
        )
        x0, x1, mid, pp, ss, sn = o
        rs, rn = exchange(ss, sn)
        ins = (flags, mid, pp, ss, sn, rs, rn, v[3], x0, x1, w2, wh2, w3, rf)
        o = call(
            functools.partial(fwd_last_body, half),
            ins,
            [SM] + [VM] * (len(ins) - 1),
            [row3(nf)] * 2 + [sds(nf, 12, 2 * PAD, lev)],
        )
        return (x0, x1, o[0], o[1]), o[2]

    def turn(xs, eg, dd, scale, row=None):
        eg = swap(eg)
        x0, x1, x2, x3 = xs
        nf = x3.shape[0]
        carry = row is not None
        ins = (flags, scale, x3, x2, eg, dd[3], dd[2], w3, w2, ra)
        ins += (row,) if carry else ()
        o = call(
            functools.partial(turn_body, carry),
            ins,
            [SM] * 2 + [VM] * (len(ins) - 2),
            state_of(nf, 2) + [sds(1, lev) if carry else part],
        )
        r = call(
            rest_body,
            (scale, x0, x1, x2, eg, dd[0], dd[1], dd[2]),
            [SM] + [VM] * 7,
            [row3(nf)] * 3 + ([] if carry else [part]),
        )
        return tuple(o[:4]), tuple(r[:3]), (o[4] if carry else (o[4], r[3]))

    def norm(v):
        return call(norm_body, tuple(v), [VM] * 4, [part])[0]

    chains = []
    for nf, gg, dd in groups:
        state = tuple(
            call(
                turn_first_body,
                (flags, gg[3], gg[2], w3, w2, ra),
                [SM] + [VM] * 5,
                state_of(nf, 2),
            )
        )
        g3, g2, state = adj_mid(state, gg[2], gg[1], gg[0])
        g0, g1, state = adj_last(state, gg[0], True)
        g = (g0, g1, g2, g3)
        xs, eg = forward(state, g)
        state, fs, bg = turn(xs, eg, dd, sig_arr)
        z3, z2, state = adj_mid(state, fs[2], fs[1], fs[0])
        z0, z1, state = adj_last(state, fs[0], True)
        z = (z0, z1, z2, z3)
        xs, eg = forward(state, z)
        chains.append((g, z, xs, eg, norm(g), bg, norm(z)))
    ins = [ch[4] for ch in chains] + [q for ch in chains for q in ch[5]]
    ins += [ch[6] for ch in chains]
    for ch, (_, _, dd) in zip(chains, groups):
        ins += list(ch[2]) + list(dd)
    row = call(
        functools.partial(sums_body, len(chains)), tuple(ins), [VM] * len(ins), [sds(1, lev)]
    )[0]
    row = call(add_body, (row, swap(row)), [VM] * 2, [sds(1, lev)], flops=1e5)[0]
    states = []
    for ch, (nf, gg, dd) in zip(chains, groups):
        state, fs, row = turn(ch[2], ch[3], dd, one_arr, row)
        states.append((state, fs))
    row = ring_sum(ring_sum(row, 1), 4)
    mids = []
    for state, fs in states:
        w3z, w2z, state, row = adj_mid(state, fs[2], fs[1], fs[0], row)
        mids.append((w3z, w2z, state, fs))
    row = ring_sum(row, 16)
    weights = call(solve_body, (span, row), [SM, VM], [sds(1, lev)], flops=1e5)[0]

    g, z = chains[0][0], chains[0][1]
    w3z, w2z, state, fs = mids[0]
    w0z, w1z, _ = adj_last(state, fs[0], False)
    w = (w0z, w1z, w2z, w3z)
    shape = sds(2, FIELDS, 3, half, lev)

    def other(v):
        return swap(
            call(outbound_body, (c_arr,) + tuple(v), [SM] + [VM] * 4, [shape])[0]
        )

    ins = (c_arr, weights) + tuple(g) + tuple(z) + w + (other(g), other(z), other(w))
    full = (2, FIELDS, 3, cols, lev)
    return call(
        functools.partial(final_body, half),
        ins,
        [SM] + [VM] * (len(ins) - 1),
        [sds(2, 1, FIELDS, 3, cols, lev)] * 2,
        scratch=[
            pltpu.VMEM(full, F32),
            pltpu.VMEM(full, F32),
            pltpu.SemaphoreType.DMA((4 * FIELDS,)),
        ],
        out_specs=[pl.BlockSpec(memory_space=pl.ANY)] * 2,
        vmem=12 * 2**20,
    )


def solution(mesh):
    in_specs = (
        P("tm", "space", None, None, None, None),
        P(),
        P("tm", "space", None, None, None),
        P("tm", "space", None, None, None),
        P("tm", "space", None, None),
        P("tm", "space", None, None),
        P("tm", "space", None),
    )
    out_specs = (P("tm", "space", None, None, None, None), P("tm", "space", None, None, None, None))
    return jax.shard_map(
        per_device, mesh=mesh, in_specs=in_specs, out_specs=out_specs, check_vma=False
    )
```
